32 devices in a mesh: gx: 8 (over y, x, core), gy: 4 (over z).
Axes of the slice: x: 2, y: 2, z: 4, core: 2. Of those that a mesh axis runs over, the one named last changes fastest.
Arguments:
- initial_thermal_state: float32 [64, 32, 16, 256], P('gx', 'gy'), may hold values from -4 to 4
- logarithmic_diffusivity: float32 [64, 32, 16, 256], P('gx', 'gy'), may hold values from -2 to 2
- rock_class_code: int32 [64, 32, 16], P('gx', 'gy'), may hold values from 0 to 7
- rock_class_diffusivity: float32 [8], replicated, may hold values from 0.004 to 0.016
- advection_courant: float32 [16], replicated, may hold values from 0 to 0.25
- probe_locations: int32 [1024], P(('gx', 'gy')), may hold values from 0 to 1023
- observed_readings: float32 [1024], P(('gx', 'gy')), may hold values from -4 to 4
- probe_noise_deviation: float32 [1024], P(('gx', 'gy')), may hold values from 0.1 to 1
- random_starters: int32 [256], replicated, may hold values from 0 to 65520
Outputs:
- temperature_final: float32 [64, 32, 16, 256], P('gx', 'gy')
- cond_updated: float32 [64, 32, 16, 256], P('gx', 'gy')
The draws below stay inside these ranges and needn't reach their ends.
Inputs may be any that keep to these rules, and one draw needn't show every extreme that they name: probe_locations[j] is a cell (x' 8 + y') * 16 + z of the tile of device j // 32, devices ordered with gy fastest.
All inputs are finite; a program needn't handle non-finite values.
Results may differ from the reference program's by a relative error of at most 0.00017.
Values sent between devices are 32-bit elements; how exact they have to be, the bound alone decides.
No kernel may reach another device: no remote copies, remote signals or barrier semaphores. Data moves between devices by JAX's collectives and lax.ppermute only.
A program may use at most 64 MiB of HBM per device.

```python
import math
import jax
import jax.numpy as jnp
from jax import lax

CX = 8
CY = 8
VERTICAL_STRATA = 16
ENSEMBLE_SIZE = 256
NF = 8
OBS_DEV = 32
GRID_SPAN_EAST = 64
GRID_SPAN_NORTH = 32
NOBS = 1024
N_GX = 8
N_GY = 4


def touch_ends(values, stream_key, low, largest):
    index_at = [jax.random.randint(jax.random.fold_in(stream_key, axis), (), 0, length) for axis, length in enumerate(values.shape)]
    main_axis = values.shape.index(max(values.shape))
    beside = index_at[:main_axis] + [(index_at[main_axis] + 1) % values.shape[main_axis]] + index_at[main_axis + 1:]
    return values.at[tuple(index_at)].set(low).at[tuple(beside)].set(largest)


def block_levels(key, dims, split, low, top_value):
    gain, own = 1.0, jax.random.fold_in(key, 6)
    for dim, parts in split:
        heights = jnp.exp(jax.random.uniform(jax.random.fold_in(own, dim), (parts,), jnp.float32, low / len(split), top_value / len(split)))
        gain = gain * jnp.repeat(heights, dims[dim] // parts).reshape([-1 if axis == dim else 1 for axis in range(len(dims))])
    return gain


def centred(key, shape, deviation, reach, cuts=(), held_as=jnp.bfloat16):
    result = deviation * jax.random.normal(key, shape, jnp.float32)
    if cuts:
        result = result * block_levels(key, shape, cuts, -0.22, 0.18)
    return jnp.clip(result, -reach, reach).astype(held_as)


def setup_inputs(seed: int = 0) -> dict:
    arg_keys = jax.random.split(jax.random.key(seed), 10)
    initial_thermal_state = centred(arg_keys[0], (GRID_SPAN_EAST, GRID_SPAN_NORTH, VERTICAL_STRATA, ENSEMBLE_SIZE), 1.0, 4.0, ((0, 8), (1, 4)), jnp.float32)
    logarithmic_diffusivity = centred(arg_keys[1], (GRID_SPAN_EAST, GRID_SPAN_NORTH, VERTICAL_STRATA, ENSEMBLE_SIZE), 0.5, 2.0, ((0, 8), (1, 4)), jnp.float32)
    rock_class_code = touch_ends(jax.random.randint(arg_keys[2], (GRID_SPAN_EAST, GRID_SPAN_NORTH, VERTICAL_STRATA), 0, NF), jax.random.fold_in(arg_keys[2], 1), 0, NF - 1).astype(jnp.int32)
    rock_class_diffusivity = jnp.clip(jnp.exp(jax.random.uniform(arg_keys[3], (NF,), jnp.float32, math.log(0.004), math.log(0.016))), 0.004, 0.016)
    advection_courant = jnp.clip(jax.random.uniform(arg_keys[4], (VERTICAL_STRATA,), jnp.float32, 0.0, 0.25), 0.0, 0.25)
    probe_locations = touch_ends(jax.random.randint(arg_keys[5], (NOBS,), 0, CX * CY * VERTICAL_STRATA), jax.random.fold_in(arg_keys[5], 1), 0, (CX * CY * VERTICAL_STRATA) - 1).astype(jnp.int32)
    observed_readings = centred(arg_keys[6], (NOBS,), 1.0, 4.0, ((0, 32),), jnp.float32)
    probe_noise_deviation = jnp.clip(jnp.exp(math.log(1.0) - 2.3025851 * jax.random.uniform(arg_keys[7], (NOBS,), jnp.float32) ** block_levels(arg_keys[7], (NOBS,), ((0, 32),), -0.2, 0.2)), 0.1, 1.0)
    random_starters = touch_ends(jax.random.randint(arg_keys[8], (ENSEMBLE_SIZE,), 0, 65521), jax.random.fold_in(arg_keys[8], 1), 0, 65520).astype(jnp.int32)
    return {"initial_thermal_state": initial_thermal_state, "logarithmic_diffusivity": logarithmic_diffusivity, "rock_class_code": rock_class_code, "rock_class_diffusivity": rock_class_diffusivity, "advection_courant": advection_courant, "probe_locations": probe_locations, "observed_readings": observed_readings, "probe_noise_deviation": probe_noise_deviation, "random_starters": random_starters}


inflation = 4.0

def window(field, shift_x, shift_y, shift_z):
    return field[1 + shift_x:field.shape[0] - 1 + shift_x, 1 + shift_y:field.shape[1] - 1 + shift_y, 1 + shift_z:field.shape[2] - 1 + shift_z]

def advance_in_time(padded_temp, padded_diffusivity, advection_courant):
    temp_z = jnp.pad(padded_temp, ((0, 0), (0, 0), (1, 1), (0, 0)))
    cond_z = jnp.pad(padded_diffusivity, ((0, 0), (0, 0), (1, 1), (0, 0)))
    center = window(temp_z, 0, 0, 0)
    cond_center = window(cond_z, 0, 0, 0)
    change = jnp.zeros_like(center)
    for shift_x, shift_y, shift_z in ((1, 0, 0), (-1, 0, 0), (0, 1, 0), (0, -1, 0), (0, 0, 1), (0, 0, -1)):
        change = change + 0.5 * (cond_center + window(cond_z, shift_x, shift_y, shift_z)) * (window(temp_z, shift_x, shift_y, shift_z) - center)
    upwind = center - window(temp_z, -1, 0, 0)
    return center + change - advection_courant[:, None] * upwind

def perturbation(obs_index, random_starters):
    first = random_starters * 7919 % 65521
    second = obs_index * 331 % 65521
    hashed = (first[None, :] * (second[:, None] % 32749) + first[None, :] + second[:, None]) % 65521
    uniform_value = (hashed.astype(jnp.float32) + 0.5) / 65521.0
    return jnp.sqrt(3.0) * (2.0 * uniform_value - 1.0)

def reference(initial_thermal_state, logarithmic_diffusivity, rock_class_code, rock_class_diffusivity, advection_courant, probe_locations, observed_readings, probe_noise_deviation, random_starters):
    levels = jnp.arange(NF, dtype=jnp.int32)
    base_cond = lax.optimization_barrier(jnp.sum((rock_class_code[..., None] == levels).astype(jnp.float32) * rock_class_diffusivity, axis=-1))
    thermal_spreading_step = base_cond[..., None] * jnp.exp(logarithmic_diffusivity)
    ghost_margin_depth = ((1, 1), (1, 1), (0, 0), (0, 0))
    padded_diffusivity = jnp.pad(thermal_spreading_step, ghost_margin_depth)
    interior_slice = advance_in_time(jnp.pad(initial_thermal_state, ghost_margin_depth), padded_diffusivity, advection_courant)
    final = advance_in_time(jnp.pad(interior_slice, ghost_margin_depth), padded_diffusivity, advection_courant)
    tiles = final.reshape(N_GX, CX, N_GY, CY, VERTICAL_STRATA, ENSEMBLE_SIZE).transpose(0, 2, 1, 3, 4, 5).reshape(N_GX * N_GY, CX * CY * VERTICAL_STRATA, ENSEMBLE_SIZE)
    cell_index = probe_locations.reshape(N_GX * N_GY, OBS_DEV)[:, :, None]
    predicted = jnp.take_along_axis(tiles, cell_index, axis=1).reshape(NOBS, ENSEMBLE_SIZE)
    scale = jnp.sqrt(jnp.float32(ENSEMBLE_SIZE - 1))
    spread = (predicted - lax.optimization_barrier(jnp.mean(predicted, axis=1, keepdims=True))) / (probe_noise_deviation[:, None] * scale)
    noise = perturbation(jnp.arange(NOBS, dtype=jnp.int32), random_starters)
    misfit = (observed_readings[:, None] + jnp.sqrt(inflation) * probe_noise_deviation[:, None] * noise - predicted) / probe_noise_deviation[:, None]
    gram = jnp.dot(spread.T, spread, precision=lax.Precision.HIGHEST)
    cross = jnp.dot(spread.T, misfit, precision=lax.Precision.HIGHEST)
    system = gram + inflation * jnp.eye(ENSEMBLE_SIZE, dtype=jnp.float32)
    lower_factor = jnp.linalg.cholesky(system)
    halfway = lax.linalg.triangular_solve(lower_factor, cross, left_side=True, lower=True)
    weights = lax.linalg.triangular_solve(lower_factor, halfway, left_side=True, lower=True, transpose_a=True)
    anomalies = ((logarithmic_diffusivity - lax.optimization_barrier(jnp.mean(logarithmic_diffusivity, axis=-1, keepdims=True))) / scale).reshape(-1, ENSEMBLE_SIZE)
    updated = logarithmic_diffusivity.reshape(-1, ENSEMBLE_SIZE) + jnp.dot(anomalies, weights, precision=lax.Precision.HIGHEST)
    return (final, updated.reshape(logarithmic_diffusivity.shape))
```

```python
import jax
import jax.numpy as jnp
from jax import lax
from jax.experimental import pallas as pl
from jax.experimental.pallas import tpu as pltpu
from jax.sharding import PartitionSpec as P

inflation = 4.0
HIGHEST = lax.Precision.HIGHEST


def swap_pairs(count, first):
    pairs = []
    for i in range(first, count - 1, 2):
        pairs += [(i, i + 1), (i + 1, i)]
    return pairs


def outer_layers(cells, axis, dim):
    count = lax.axis_size(axis)
    even = lax.axis_index(axis) % 2 == 0
    head = lax.slice_in_dim(cells, 0, 1, axis=dim)
    tail = lax.slice_in_dim(cells, cells.shape[dim] - 1, cells.shape[dim], axis=dim)
    first = lax.ppermute(jnp.where(even, tail, head), axis, swap_pairs(count, 0))
    second = lax.ppermute(jnp.where(even, head, tail), axis, swap_pairs(count, 1))
    return jnp.where(even, second, first), jnp.where(even, first, second)


def with_layers(cells, layers_x, layers_y, dim):
    wide = jnp.concatenate([layers_x[0], cells, layers_x[1]], axis=dim)
    pads = [(0, 0)] * cells.ndim
    pads[dim] = (1, 1)
    south, north = (jnp.pad(layer, pads) for layer in layers_y)
    return jnp.concatenate([south, wide, north], axis=dim + 1)


def window(field, shift_x, shift_y, shift_z):
    return field[
        1 + shift_x : field.shape[0] - 1 + shift_x,
        1 + shift_y : field.shape[1] - 1 + shift_y,
        1 + shift_z : field.shape[2] - 1 + shift_z,
    ]


def advance_in_time(padded_temp, padded_diffusivity, advection_courant):
    temp_z = jnp.pad(padded_temp, ((0, 0), (0, 0), (1, 1), (0, 0)))
    cond_z = jnp.pad(padded_diffusivity, ((0, 0), (0, 0), (1, 1), (0, 0)))
    center = window(temp_z, 0, 0, 0)
    cond_center = window(cond_z, 0, 0, 0)
    change = jnp.zeros_like(center)
    for shift_x, shift_y, shift_z in (
        (1, 0, 0),
        (-1, 0, 0),
        (0, 1, 0),
        (0, -1, 0),
        (0, 0, 1),
        (0, 0, -1),
    ):
        change = change + 0.5 * (cond_center + window(cond_z, shift_x, shift_y, shift_z)) * (
            window(temp_z, shift_x, shift_y, shift_z) - center
        )
    upwind = center - window(temp_z, -1, 0, 0)
    return center + change - advection_courant[:, None] * upwind


def modulo(value, divisor):
    quotient = (value.astype(jnp.float32) * (1.0 / divisor)).astype(jnp.int32)
    rest = value - quotient * divisor
    rest = jnp.where(rest < 0, rest + divisor, rest)
    return jnp.where(rest >= divisor, rest - divisor, rest)


def perturbation(obs_index, random_starters):
    first = random_starters * 7919 % 65521
    second = obs_index * 331 % 65521
    hashed = modulo(
        first[None, :] * (second[:, None] % 32749) + first[None, :] + second[:, None], 65521
    )
    uniform_value = (hashed.astype(jnp.float32) + 0.5) / 65521.0
    return jnp.sqrt(3.0) * (2.0 * uniform_value - 1.0)


def plan_exchange(axes, rows, limit):
    gathers, sums, stride = [], [], 1
    for axis in axes:
        count = lax.axis_size(axis)
        bits = [1 << b for b in range(count.bit_length() - 1)]
        while bits:
            if len(bits) > 1 and rows * 4 <= limit:
                low, high = bits[-2], bits[-1]
                gathers.append((axis, stride, (low, high, low | high)))
                rows, bits = rows * 4, bits[:-2]
            elif rows * 2 <= limit:
                gathers.append((axis, stride, (bits.pop(),)))
                rows *= 2
            else:
                sums.append((axis, bits.pop()))
        stride *= count
    return gathers, sums


def swap(block, axis, step):
    return lax.ppermute(block, axis, [(i, i ^ step) for i in range(lax.axis_size(axis))])


def gather_blocks(block, owner, gathers):
    owners = owner[None]
    for axis, stride, steps in gathers:
        block = jnp.concatenate([block] + [swap(block, axis, step) for step in steps])
        owners = jnp.concatenate([owners] + [owners ^ (step * stride) for step in steps])
    return block, owners


def product(a, b, over_a=1, over_b=0):
    return lax.dot_general(
        a, b, (((over_a,), (over_b,)), ((), ())), precision=HIGHEST,
        preferred_element_type=jnp.float32,
    )


def inverse(block):
    size = block.shape[0]
    lane = lax.broadcasted_iota(jnp.int32, (size, size), 1)
    row_index = lax.broadcasted_iota(jnp.int32, (size, size), 0)

    def eight(_, held):
        for p in range(8):
            row = held[p : p + 1, :]
            column = jnp.broadcast_to(held[:, p : p + 1], (size, size))
            pivot = 1.0 / column[p : p + 1, :]
            scaled = jnp.where(lane[:1] == p, pivot, row * pivot)
            column = jnp.where(row_index == p, -1.0, column)
            held = jnp.where((lane == p) | (row_index == p), 0.0, held) - column * scaled
        held = jnp.concatenate([held[8:], held[:8]], 0)
        return pltpu.roll(held, size - 8, 1)

    return lax.fori_loop(0, size // 8, eight, block)


def products(scale, scaled_ref, noise_ref, out_ref):
    scaled = scaled_ref[...]
    members = scaled.shape[1]
    spread = scaled - jnp.sum(scaled, axis=1, keepdims=True) * (1.0 / members)
    misfit = noise_ref[...] - scale * scaled
    out_ref[:, :members] = product(spread, spread, 0, 0)
    out_ref[:, members:] = product(spread, misfit, 0, 0)


def solve(sums_ref, weights_ref):
    members = weights_ref.shape[0]
    half = members // 2
    diagonal = lax.broadcasted_iota(jnp.int32, (half, half), 0) == lax.broadcasted_iota(
        jnp.int32, (half, half), 1
    )
    shift = jnp.where(diagonal, inflation, 0.0)
    upper = product(inverse(sums_ref[:half, :half] + shift), sums_ref[:half, half:])
    lower = sums_ref[half:, half:] - product(sums_ref[half:, :half], upper)
    second = product(inverse(lower[:, :half] + shift), lower[:, half:])
    weights_ref[:half] = upper[:, half:] - product(upper[:, :half], second)
    weights_ref[half:] = second


def smoother(scale, scaled_ref, noise_ref, weights_ref, sums_ref):
    products(scale, scaled_ref, noise_ref, sums_ref)
    solve(sums_ref, weights_ref)


def ensemble_weights(scale, scaled, noise, sums):
    members = scaled.shape[1]
    pair = (members, 2 * members)
    weights = jax.ShapeDtypeStruct((members, members), jnp.float32)
    if not sums:
        return pl.pallas_call(
            lambda *refs: smoother(scale, *refs),
            out_shape=weights,
            scratch_shapes=[pltpu.VMEM(pair, jnp.float32)],
            name="smoother",
        )(scaled, noise)
    total = pl.pallas_call(
        lambda *refs: products(scale, *refs),
        out_shape=jax.ShapeDtypeStruct(pair, jnp.float32),
        name="products",
    )(scaled, noise)
    for axis, step in sums:
        total = total + swap(total, axis, step)
    return pl.pallas_call(solve, out_shape=weights, name="solve")(total)


def shards(
    initial_thermal_state,
    logarithmic_diffusivity,
    rock_class_code,
    rock_class_diffusivity,
    advection_courant,
    probe_locations,
    observed_readings,
    probe_noise_deviation,
    random_starters,
):
    members = initial_thermal_state.shape[-1]
    levels = jnp.arange(rock_class_diffusivity.shape[0], dtype=jnp.int32)
    base_cond = jnp.sum(
        (rock_class_code[..., None] == levels).astype(jnp.float32) * rock_class_diffusivity, axis=-1
    )
    cond = base_cond[..., None] * jnp.exp(logarithmic_diffusivity)
    both = jnp.stack([initial_thermal_state, cond])
    extended = with_layers(both, outer_layers(both, "gx", 1), outer_layers(both, "gy", 2), 1)
    middle = advance_in_time(extended[0], extended[1], advection_courant)
    padded_middle = with_layers(
        middle, outer_layers(middle, "gx", 0), outer_layers(middle, "gy", 1), 0
    )
    final = advance_in_time(padded_middle, extended[1], advection_courant)
    predicted = jnp.take(final.reshape(-1, members), probe_locations, axis=0)
    scale = (members - 1) ** 0.5
    scaled = (predicted - observed_readings[:, None]) / (probe_noise_deviation[:, None] * scale)
    obs_count = probe_locations.shape[0]
    gathers, sums = plan_exchange(("gy", "gx"), obs_count, 4 * members)
    everyone, owners = gather_blocks(scaled, lax.axis_index(("gx", "gy")), gathers)
    obs_index = (
        owners[:, None] * obs_count + jnp.arange(obs_count, dtype=jnp.int32)[None, :]
    ).reshape(-1)
    noise = inflation**0.5 * perturbation(obs_index, random_starters)
    weights = ensemble_weights(scale, everyone, noise, sums)
    anomalies = (
        (logarithmic_diffusivity - jnp.mean(logarithmic_diffusivity, axis=-1, keepdims=True))
        / scale
    ).reshape(-1, members)
    updated = logarithmic_diffusivity.reshape(-1, members) + product(anomalies, weights)
    return (final, updated.reshape(logarithmic_diffusivity.shape))


def solution(mesh):
    placed = (
        P("gx", "gy", None, None),
        P("gx", "gy", None, None),
        P("gx", "gy", None),
        P(),
        P(),
        P(("gx", "gy")),
        P(("gx", "gy")),
        P(("gx", "gy")),
        P(),
    )
    return jax.shard_map(
        shards,
        mesh=mesh,
        in_specs=placed,
        out_specs=(P("gx", "gy", None, None), P("gx", "gy", None, None)),
        check_vma=False,
    )
```

```python
import functools

import jax
import jax.numpy as jnp
from jax import lax
from jax.experimental import pallas as pl
from jax.experimental.pallas import tpu as pltpu
from jax.sharding import PartitionSpec as P

inflation = 4.0
HIGHEST = lax.Precision.HIGHEST
VMEM = pl.BlockSpec(memory_space=pltpu.VMEM)
SMEM = pl.BlockSpec(memory_space=pltpu.SMEM)


def f32(*shape):
    return jax.ShapeDtypeStruct(shape, jnp.float32)


def call(kernel, name, outs, specs, args, scratch=(), flops=0):
    moved = sum(4 * a.size for a in args)
    return pl.pallas_call(
        kernel,
        out_shape=outs,
        in_specs=specs,
        out_specs=jax.tree.map(lambda _: VMEM, outs),
        scratch_shapes=scratch,
        compiler_params=pltpu.CompilerParams(vmem_limit_bytes=24 << 20),
        cost_estimate=pl.CostEstimate(flops=flops, bytes_accessed=moved, transcendentals=0),
        name=name,
    )(*args)


def swap_pairs(count, first):
    pairs = []
    for i in range(first, count - 1, 2):
        pairs += [(i, i + 1), (i + 1, i)]
    return pairs


def is_even(axis):
    return lax.rem(lax.axis_index(axis), 2) == 0


def exchange(faces):
    got = []
    for axis, first, face in zip(("gx", "gx", "gy", "gy"), (0, 1, 0, 1), faces):
        got.append(lax.ppermute(face, axis, swap_pairs(lax.axis_size(axis), first)))
    return got


def store_faces(field_ref, rows, put):
    span_x, span_y = rows
    for axis, base in (("gx", 0), ("gy", 2)):
        even = is_even(axis)
        last = (span_x if axis == "gx" else span_y) - 1
        for n in range(2):
            at = jnp.where(even, last, 0) if n == 0 else jnp.where(even, 0, last)
            for k in range(span_y if axis == "gx" else span_x):
                cell = at * span_y + k if axis == "gx" else k * span_y + at
                put(base + n, k, field_ref[cell])


def prepare(rows, t_ref, log_ref, code_ref, rock_ref, h_ref, *rest):
    face_refs, turned = rest[:4], rest[4]
    span_x, span_y = rows
    depth, members = t_ref.shape[1:]
    turned[...] = jnp.zeros_like(turned)
    for x in range(span_x):
        code = code_ref[x]
        base = jnp.zeros(code.shape, jnp.float32)
        for level in range(rock_ref.shape[0]):
            base = jnp.where(code == level, 0.5 * rock_ref[level], base)
        turned[x * span_y : (x + 1) * span_y, :depth] = base
    columns = jnp.transpose(turned[...])[:depth]
    for cell in range(span_x * span_y):
        base = jnp.broadcast_to(columns[:, cell : cell + 1], (depth, members))
        h_ref[cell] = base * jnp.exp(log_ref[cell])

    def put(field):
        def store(n, k, layer):
            face_refs[n][field, k] = layer

        return store

    store_faces(t_ref, rows, put(0))
    store_faces(h_ref, rows, put(1))


def advance(rows, courant_ref, u_ref, h_ref, u_faces, h_faces, write):
    span_x, span_y = rows
    shape = u_ref.shape[1:]
    depth = shape[0]
    level = lax.broadcasted_iota(jnp.int32, shape, 0)
    courant = jnp.zeros(shape, jnp.float32)
    for z in range(depth):
        courant = jnp.where(level == z, courant_ref[z], courant)
    even_x, even_y = is_even("gx"), is_even("gy")

    def beyond(faces, axis, side, k):
        even = even_x if axis == 0 else even_y
        first, second = faces(2 * axis, k), faces(2 * axis + 1, k)
        return jnp.where(even, second, first) if side < 0 else jnp.where(even, first, second)

    def at(ref, faces, x, y):
        if x < 0 or x == span_x:
            return beyond(faces, 0, -1 if x < 0 else 1, y)
        if y < 0 or y == span_y:
            return beyond(faces, 1, -1 if y < 0 else 1, x)
        return ref[x * span_y + y]

    for x in range(span_x):
        south = None
        for y in range(span_y):
            u, h = u_ref[x * span_y + y], h_ref[x * span_y + y]

            def flow(i, j):
                step = at(u_ref, u_faces, i, j) - u
                return step, (h + at(h_ref, h_faces, i, j)) * step

            rise = jnp.where(level == depth - 1, 0.0, pltpu.roll(u, depth - 1, 0)) - u
            lift = (h + jnp.where(level == depth - 1, 0.0, pltpu.roll(h, depth - 1, 0))) * rise
            sink = jnp.where(level == 0, h * u, pltpu.roll(lift, 1, 0))
            west, from_west = flow(x - 1, y)
            from_east = flow(x + 1, y)[1]
            from_north = flow(x, y + 1)[1]
            from_south = flow(x, y - 1)[1] if south is None else south
            south = -from_north
            change = (from_east + from_west) + (from_north + from_south) + (lift - sink)
            write(x * span_y + y, u + change + courant * west)


def halfway(rows, courant_ref, t_ref, h_ref, *rest):
    got, middle_ref, face_refs = rest[:4], rest[4], rest[5:9]

    def write(cell, value):
        middle_ref[cell] = value

    advance(
        rows, courant_ref, t_ref, h_ref,
        lambda n, k: got[n][0, k], lambda n, k: got[n][1, k], write,
    )

    def put(n, k, layer):
        face_refs[n][k] = layer

    store_faces(middle_ref, rows, put)


def observe(rows, courant_ref, cells_ref, reading_ref, factor_ref, u_ref, h_ref, *rest):
    got_u, got_h, final_ref, scaled_ref = rest[:4], rest[4:8], rest[8], rest[9]
    depth = u_ref.shape[1]

    def write(cell, value):
        final_ref[cell * depth : (cell + 1) * depth, :] = value

    advance(
        rows, courant_ref, u_ref, h_ref,
        lambda n, k: got_u[n][k], lambda n, k: got_h[n][1, k], write,
    )
    for j in range(scaled_ref.shape[0]):
        row = final_ref[pl.ds(cells_ref[j], 1), :]
        scaled_ref[j : j + 1, :] = (row - reading_ref[j]) * factor_ref[j]


def modulo(value, divisor):
    quotient = (value.astype(jnp.float32) * (1.0 / divisor)).astype(jnp.int32)
    rest = value - quotient * divisor
    rest = jnp.where(rest < 0, rest + divisor, rest)
    return jnp.where(rest >= divisor, rest - divisor, rest)


def perturbation(obs_index, random_starters):
    first = random_starters * 7919 % 65521
    second = obs_index * 331 % 65521
    hashed = modulo(
        first[None, :] * (second[:, None] % 32749) + first[None, :] + second[:, None], 65521
    )
    uniform_value = (hashed.astype(jnp.float32) + 0.5) / 65521.0
    return jnp.sqrt(3.0) * (2.0 * uniform_value - 1.0)


def plan_exchange(axes, rows, limit):
    gathers, sums, stride = [], [], 1
    for axis in axes:
        count = lax.axis_size(axis)
        bits = [1 << b for b in range(count.bit_length() - 1)]
        while bits:
            if len(bits) > 1 and rows * 4 <= limit:
                low, high = bits[-2], bits[-1]
                gathers.append((axis, stride, (low, high, low | high)))
                rows, bits = rows * 4, bits[:-2]
            elif rows * 2 <= limit:
                gathers.append((axis, stride, (bits.pop(),)))
                rows *= 2
            else:
                sums.append((axis, bits.pop()))
        stride *= count
    return gathers, sums


def swap(block, axis, step):
    return lax.ppermute(block, axis, [(i, i ^ step) for i in range(lax.axis_size(axis))])


def pack(*refs):
    start = 0
    for ref in refs[:-1]:
        refs[-1][start : start + ref.shape[0], :] = ref[...]
        start += ref.shape[0]


def gather_blocks(block, owner, gathers):
    pieces, owners = [block], owner[None]
    for axis, stride, steps in gathers:
        if len(steps) > 1 and len(pieces) > 1:
            rows = sum(piece.shape[0] for piece in pieces)
            pieces = [
                call(pack, "pack", f32(rows, block.shape[1]), [VMEM] * len(pieces), pieces)
            ]
        pieces = pieces + [swap(piece, axis, step) for step in steps for piece in pieces]
        owners = jnp.concatenate([owners] + [owners ^ (step * stride) for step in steps])
    return pieces, owners


def product(a, b, over_a=1, over_b=0):
    return lax.dot_general(
        a, b, (((over_a,), (over_b,)), ((), ())), precision=HIGHEST,
        preferred_element_type=jnp.float32,
    )


def inverse(block):
    size = block.shape[0]
    shape = (8, size)
    lane = lax.broadcasted_iota(jnp.int32, shape, 1)
    sub = lax.broadcasted_iota(jnp.int32, shape, 0)
    count = size // 8
    rows = [block[8 * i : 8 * i + 8, :] for i in range(count)]
    for g in range(count):
        first = 8 * g
        inside = (lane >= first) & (lane < first + 8)
        columns = [
            jnp.broadcast_to(rows[g][:, first + q : first + q + 1], shape) for q in range(8)
        ]
        held = jnp.where(inside, jnp.where(lane - first == sub, 1.0, 0.0), rows[g])
        for p in range(8):
            pivot = 1.0 / columns[p][p : p + 1, :]
            for q in range(p + 1, 8):
                scaled = columns[q][p : p + 1, :] * pivot
                columns[q] = jnp.where(sub == p, scaled, columns[q] - columns[p] * scaled)
            scaled = held[p : p + 1, :] * pivot
            held = jnp.where(sub == p, scaled, held - columns[p] * scaled)
        rows[g] = held
        spread = [jnp.broadcast_to(held[q : q + 1, :], shape) for q in range(8)]
        for i in [*range(g + 1, count), *range(g)]:
            left = jnp.where(inside, 0.0, rows[i])
            for q in range(8):
                left -= jnp.broadcast_to(rows[i][:, first + q : first + q + 1], shape) * spread[q]
            rows[i] = left
    return jnp.concatenate(rows, 0)


def products(scale, piece_refs, noise_ref, out_ref):
    scaled = jnp.concatenate([ref[...] for ref in piece_refs])
    members = scaled.shape[1]
    spread = scaled - jnp.sum(scaled, axis=1, keepdims=True) * (1.0 / members)
    misfit = noise_ref[...] - scale * scaled
    out_ref[:, :members] = product(spread, spread, 0, 0)
    out_ref[:, members:] = product(spread, misfit, 0, 0)


def update(scale, sums_ref, log_ref, updated_ref, weights_ref):
    members = weights_ref.shape[0]
    half = members // 2
    diagonal = lax.broadcasted_iota(jnp.int32, (half, half), 0) == lax.broadcasted_iota(
        jnp.int32, (half, half), 1
    )
    shift = jnp.where(diagonal, inflation, 0.0)
    upper = product(inverse(sums_ref[:half, :half] + shift), sums_ref[:half, half:])
    lower = sums_ref[half:, half:] - product(sums_ref[half:, :half], upper)
    second = product(inverse(lower[:, :half] + shift), lower[:, half:])
    first = upper[:, half:] - product(upper[:, :half], second)
    mean = (
        jnp.sum(first, axis=0, keepdims=True) + jnp.sum(second, axis=0, keepdims=True)
    ) * (1.0 / members)
    weights_ref[:half] = (first - mean) * (1.0 / scale)
    weights_ref[half:] = (second - mean) * (1.0 / scale)
    updated_ref[...] = log_ref[...] + product(log_ref[...], weights_ref[...])


def smooth(scale, *refs):
    *piece_refs, noise_ref, log_ref, updated_ref, sums_ref, weights_ref = refs
    products(scale, piece_refs, noise_ref, sums_ref)
    update(scale, sums_ref, log_ref, updated_ref, weights_ref)


def assimilate(scale, pieces, noise, log_rows, sums):
    members = noise.shape[1]
    pair = (members, 2 * members)
    weights = pltpu.VMEM((members, members), jnp.float32)
    updated = f32(*log_rows.shape)
    if not sums:
        args = [*pieces, noise, log_rows]
        return call(
            functools.partial(smooth, scale), "smooth", updated, [VMEM] * len(args), args,
            scratch=[pltpu.VMEM(pair, jnp.float32), weights], flops=10**9,
        )
    args = [*pieces, noise]
    total = call(
        lambda *refs: products(scale, refs[:-2], *refs[-2:]), "products", f32(*pair),
        [VMEM] * len(args), args, flops=10**9,
    )
    for axis, step in sums:
        total = total + swap(total, axis, step)
    return call(
        functools.partial(update, scale), "update", updated, [VMEM] * 2, [total, log_rows],
        scratch=[weights], flops=10**9,
    )


def shards(
    initial_thermal_state,
    logarithmic_diffusivity,
    rock_class_code,
    rock_class_diffusivity,
    advection_courant,
    probe_locations,
    observed_readings,
    probe_noise_deviation,
    random_starters,
):
    span_x, span_y, depth, members = initial_thermal_state.shape
    rows = (span_x, span_y)
    cells = span_x * span_y
    temperature = initial_thermal_state.reshape(cells, depth, members)
    log_cond = logarithmic_diffusivity.reshape(cells, depth, members)
    tile = f32(cells, depth, members)
    faces = [(span_y, depth, members)] * 2 + [(span_x, depth, members)] * 2
    half_cond, *sent = call(
        functools.partial(prepare, rows), "prepare",
        (tile, *(f32(2, *face) for face in faces)),
        [VMEM, VMEM, VMEM, SMEM],
        [temperature, log_cond, rock_class_code, rock_class_diffusivity],
        scratch=[pltpu.VMEM((-(-cells // 128) * 128, 128), jnp.float32)],
    )
    got = exchange(sent)
    middle, *sent = call(
        functools.partial(halfway, rows), "halfway",
        (tile, *(f32(*face) for face in faces)),
        [SMEM] + [VMEM] * 6,
        [advection_courant, temperature, half_cond, *got],
    )
    got_middle = exchange(sent)
    scale = (members - 1) ** 0.5
    obs_count = probe_locations.shape[0]
    final, scaled = call(
        functools.partial(observe, rows), "observe",
        (f32(cells * depth, members), f32(obs_count, members)),
        [SMEM] * 4 + [VMEM] * 10,
        [
            advection_courant, probe_locations, observed_readings,
            1.0 / (probe_noise_deviation * scale), middle, half_cond, *got_middle, *got,
        ],
    )
    gathers, sums = plan_exchange(("gy", "gx"), obs_count, 4 * members)
    pieces, owners = gather_blocks(scaled, lax.axis_index(("gx", "gy")), gathers)
    obs_index = (
        owners[:, None] * obs_count + jnp.arange(obs_count, dtype=jnp.int32)[None, :]
    ).reshape(-1)
    noise = inflation**0.5 * perturbation(obs_index, random_starters)
    updated = assimilate(scale, pieces, noise, log_cond.reshape(-1, members), sums)
    shape = initial_thermal_state.shape
    return (final.reshape(shape), updated.reshape(shape))


def solution(mesh):
    placed = (
        P("gx", "gy", None, None),
        P("gx", "gy", None, None),
        P("gx", "gy", None),
        P(),
        P(),
        P(("gx", "gy")),
        P(("gx", "gy")),
        P(("gx", "gy")),
        P(),
    )
    return jax.shard_map(
        shards,
        mesh=mesh,
        in_specs=placed,
        out_specs=(P("gx", "gy", None, None), P("gx", "gy", None, None)),
        check_vma=False,
    )
```

```python
import functools

import jax
import jax.numpy as jnp
from jax import lax
from jax.experimental import pallas as pl
from jax.experimental.pallas import tpu as pltpu
from jax.sharding import PartitionSpec as P

inflation = 4.0
HIGHEST = lax.Precision.HIGHEST
VMEM = pl.BlockSpec(memory_space=pltpu.VMEM)
SMEM = pl.BlockSpec(memory_space=pltpu.SMEM)


HBM = pl.BlockSpec(memory_space=pltpu.HBM)


def f32(*shape):
    return jax.ShapeDtypeStruct(shape, jnp.float32)


def call(kernel, name, outs, specs, args, scratch=(), flops=0, out_specs=None, aliases={}):
    moved = sum(4 * a.size for a in args)
    return pl.pallas_call(
        kernel,
        out_shape=outs,
        in_specs=specs,
        out_specs=jax.tree.map(lambda _: VMEM, outs) if out_specs is None else out_specs,
        scratch_shapes=scratch,
        input_output_aliases=aliases,
        compiler_params=pltpu.CompilerParams(vmem_limit_bytes=20 << 20),
        cost_estimate=pl.CostEstimate(flops=flops, bytes_accessed=moved, transcendentals=0),
        name=name,
    )(*args)


def halo_routes(count_x, count_y):
    def flat(i, j):
        return i * count_y + j

    def turn(i, j):
        ahead = j + 1 if i % 2 == 0 else j - 1
        return (i, ahead) if 0 <= ahead < count_y else (i ^ 1, j)

    places = [(i, j) for i in range(count_x) for j in range(count_y)]
    right = [(flat(i, j), flat((i + 1) % count_x, j)) for i, j in places]
    along = [(flat(i, j), flat(*turn(i, j))) for i, j in places]
    return [right, back(right), along, back(along)]


def back(route):
    return [(b, a) for a, b in route]


def exchange(faces):
    routes = halo_routes(lax.axis_size("gx"), lax.axis_size("gy"))
    return [lax.ppermute(face, ("gx", "gy"), route) for face, route in zip(faces, routes)]


def border(rows, wanted):
    span_x, span_y = rows
    return [
        (x, y)
        for x in range(span_x)
        for y in range(span_y)
        if (x in (0, span_x - 1) or y in (0, span_y - 1)) == wanted
    ]


def is_even():
    return lax.rem(lax.axis_index("gx"), 2) == 0


def store_faces(field_ref, rows, put):
    span_x, span_y = rows
    even = is_even()
    for y in range(span_y):
        put(0, y, field_ref[(span_x - 1) * span_y + y])
        put(1, y, field_ref[y])
    for x in range(span_x):
        for route, at in (
            (2, jnp.where(even, span_y - 1, 0)),
            (3, jnp.where(even, 0, span_y - 1)),
        ):
            put(route, x, field_ref[x * span_y + at])


def conductivity(rows, cells, log_ref, columns_ref, h_ref):
    depth, members = log_ref.shape[1:]
    columns = columns_ref[...]
    for x, y in cells:
        cell = x * rows[1] + y
        base = jnp.broadcast_to(columns[:, cell : cell + 1], (depth, members))
        h_ref[cell] = base * jnp.exp(log_ref[cell])


def prepare(rows, t_hbm, log_hbm, code_hbm, rock_hbm, *rest):
    t_ref, log_ref, h_ref, columns_ref, *face_refs, turned, code_ref, rock_ref, sems = rest
    span_x, span_y = rows
    depth = t_ref.shape[1]
    copies = [
        pltpu.make_async_copy(source, target, sems.at[n])
        for n, (source, target) in enumerate(
            ((code_hbm, code_ref), (rock_hbm, rock_ref), (log_hbm, log_ref), (t_hbm, t_ref))
        )
    ]
    for copy in copies:
        copy.start()
    turned[...] = jnp.zeros_like(turned)
    copies[0].wait()
    copies[1].wait()
    for x in range(span_x):
        code = code_ref[x]
        base = jnp.zeros(code.shape, jnp.float32)
        for level in range(rock_ref.shape[0]):
            base = jnp.where(code == level, 0.5 * rock_ref[level], base)
        turned[x * span_y : (x + 1) * span_y, :depth] = base
    columns_ref[...] = jnp.transpose(turned[...])[:depth]
    copies[2].wait()
    conductivity(rows, border(rows, True), log_ref, columns_ref, h_ref)

    def put(field):
        def store(n, k, layer):
            face_refs[n][field, k] = layer

        return store

    store_faces(h_ref, rows, put(1))
    copies[3].wait()
    store_faces(t_ref, rows, put(0))


def advance(rows, cells, courant_ref, u_ref, h_ref, u_faces, h_faces, write):
    span_x, span_y = rows
    shape = u_ref.shape[1:]
    depth = shape[0]
    level = lax.broadcasted_iota(jnp.int32, shape, 0)
    courant = jnp.zeros(shape, jnp.float32)
    for z in range(depth):
        courant = jnp.where(level == z, courant_ref[z], courant)
    even = is_even()

    def beyond(faces, axis, after, k):
        name = ("gx", "gy")[axis]
        edge = lax.axis_index(name) == (lax.axis_size(name) - 1 if after else 0)
        if axis == 0:
            layer = faces(1 if after else 0, k)
        else:
            layer = jnp.where(even == after, faces(3, k), faces(2, k))
        return jnp.where(edge, 0.0, layer)

    def at(ref, faces, x, y):
        if x < 0 or x == span_x:
            return beyond(faces, 0, x > 0, y)
        if y < 0 or y == span_y:
            return beyond(faces, 1, y > 0, x)
        return ref[x * span_y + y]

    before, from_before = None, None
    for x, y in cells:
        u, h = u_ref[x * span_y + y], h_ref[x * span_y + y]

        def flow(i, j):
            step = at(u_ref, u_faces, i, j) - u
            return step, (h + at(h_ref, h_faces, i, j)) * step

        rise = jnp.where(level == depth - 1, 0.0, pltpu.roll(u, depth - 1, 0)) - u
        lift = (h + jnp.where(level == depth - 1, 0.0, pltpu.roll(h, depth - 1, 0))) * rise
        sink = jnp.where(level == 0, h * u, pltpu.roll(lift, 1, 0))
        west, from_west = flow(x - 1, y)
        from_east = flow(x + 1, y)[1]
        from_north = flow(x, y + 1)[1]
        from_south = from_before if before == (x, y - 1) else flow(x, y - 1)[1]
        before, from_before = (x, y), -from_north
        change = (from_east + from_west) + (from_north + from_south) + (lift - sink)
        write(x * span_y + y, u + change + courant * west)


def into(ref):
    def write(cell, value):
        ref[cell] = value

    return write


def middle_inside(rows, courant_ref, t_ref, log_ref, columns_ref, outer_ref, h_ref, middle_ref):
    del outer_ref
    inside = border(rows, False)
    conductivity(rows, inside, log_ref, columns_ref, h_ref)
    advance(rows, inside, courant_ref, t_ref, h_ref, None, None, into(middle_ref))


def middle_border(rows, courant_ref, t_ref, h_ref, *rest):
    got, middle_ref, face_refs = rest[:4], rest[5], rest[6:]
    advance(
        rows, border(rows, True), courant_ref, t_ref, h_ref,
        lambda n, k: got[n][0, k], lambda n, k: got[n][1, k], into(middle_ref),
    )

    def put(n, k, layer):
        face_refs[n][k] = layer

    store_faces(middle_ref, rows, put)


def final_inside(rows, courant_ref, u_ref, h_ref, final_ref):
    advance(rows, border(rows, False), courant_ref, u_ref, h_ref, None, None, into(final_ref))


def observe(rows, courant_ref, cells_ref, reading_ref, factor_ref, u_ref, h_ref, *rest):
    got_u, got_h, final_ref, scaled_ref = rest[:4], rest[4:8], rest[9], rest[10]
    depth = u_ref.shape[1]
    advance(
        rows, border(rows, True), courant_ref, u_ref, h_ref,
        lambda n, k: got_u[n][k], lambda n, k: got_h[n][1, k], into(final_ref),
    )
    for j in range(scaled_ref.shape[0]):
        cell = cells_ref[j]
        row = final_ref[lax.div(cell, depth), pl.ds(lax.rem(cell, depth), 1), :]
        scaled_ref[j : j + 1, :] = (row - reading_ref[j]) * factor_ref[j]


def modulo(value, divisor):
    quotient = (value.astype(jnp.float32) * (1.0 / divisor)).astype(jnp.int32)
    rest = value - quotient * divisor
    rest = jnp.where(rest < 0, rest + divisor, rest)
    return jnp.where(rest >= divisor, rest - divisor, rest)


def perturbation(obs_index, random_starters):
    first = random_starters * 7919 % 65521
    second = obs_index * 331 % 65521
    hashed = modulo(
        first[None, :] * (second[:, None] % 32749) + first[None, :] + second[:, None], 65521
    )
    uniform_value = (hashed.astype(jnp.float32) + 0.5) / 65521.0
    return jnp.sqrt(3.0) * (2.0 * uniform_value - 1.0)


def plan_exchange(count_x, count_y, rows, limit):
    def route(move):
        return [
            (i * count_y + j, a * count_y + b)
            for i in range(count_x)
            for j in range(count_y)
            for a, b in [move(i, j)]
        ]

    def shifted(axis, i, j, step):
        return (i ^ step, j) if axis == "gx" else (i, j ^ step)

    def across(axis, step):
        def move(i, j):
            at = i if axis == "gx" else j
            a, b = shifted(axis, i, j, step)
            return (a, b) if at < at ^ step else (a ^ 1, b)

        return route(move)

    def around(axis, low, high):
        def move(i, j):
            at = i if axis == "gx" else j
            step = low if bool(at & low) == bool(at & high) else high
            return shifted(axis, i, j, step)

        return route(move)

    gathers, sums = [], []
    for axis, count in (("gy", count_y), ("gx", count_x)):
        bits = [1 << b for b in range(count.bit_length() - 1)]
        while bits:
            if len(bits) > 1 and rows * 4 <= limit:
                high, low = bits.pop(), bits.pop()
                ring = around(axis, low, high)
                gathers.append([across(axis, low | high), ring, back(ring)])
                rows *= 4
                continue
            step = bits.pop()
            swap = route(functools.partial(shifted, axis, step=step))
            if rows * 2 <= limit:
                gathers.append([swap])
                rows *= 2
            else:
                sums.append(swap)
    return gathers, sums


def send(block, route):
    return lax.ppermute(block, ("gx", "gy"), route)


def pack(*refs):
    start = 0
    for ref in refs[:-1]:
        refs[-1][start : start + ref.shape[0], :] = ref[...]
        start += ref.shape[0]


def gather_blocks(block, gathers, devices):
    pieces, owners = [block], [[d] for d in range(devices)]
    for routes in gathers:
        if len(routes) > 1 and len(pieces) > 1:
            rows = sum(piece.shape[0] for piece in pieces)
            pieces = [
                call(pack, "pack", f32(rows, block.shape[1]), [VMEM] * len(pieces), pieces)
            ]
        pieces = pieces + [send(piece, route) for route in routes for piece in pieces]
        held = [list(own) for own in owners]
        for route in routes:
            for source, target in route:
                held[target] += owners[source]
        owners = held
    return pieces, owners


def product(a, b, over_a=1, over_b=0):
    return lax.dot_general(
        a, b, (((over_a,), (over_b,)), ((), ())), precision=HIGHEST,
        preferred_element_type=jnp.float32,
    )


def inverse(block):
    size = block.shape[0]
    shape = (8, size)
    lane = lax.broadcasted_iota(jnp.int32, shape, 1)
    sub = lax.broadcasted_iota(jnp.int32, shape, 0)
    count = size // 8
    rows = [block[8 * i : 8 * i + 8, :] for i in range(count)]
    for g in range(count):
        first = 8 * g
        inside = (lane >= first) & (lane < first + 8)
        columns = [
            jnp.broadcast_to(rows[g][:, first + q : first + q + 1], shape) for q in range(8)
        ]
        held = jnp.where(inside, jnp.where(lane - first == sub, 1.0, 0.0), rows[g])
        for p in range(8):
            pivot = 1.0 / columns[p][p : p + 1, :]
            for q in range(p + 1, 8):
                scaled = columns[q][p : p + 1, :] * pivot
                columns[q] = jnp.where(sub == p, scaled, columns[q] - columns[p] * scaled)
            scaled = held[p : p + 1, :] * pivot
            held = jnp.where(sub == p, scaled, held - columns[p] * scaled)
        rows[g] = held
        spread = [jnp.broadcast_to(held[q : q + 1, :], shape) for q in range(8)]
        for i in [*range(g + 1, count), *range(g)]:
            left = jnp.where(inside, 0.0, rows[i])
            for q in range(8):
                left -= jnp.broadcast_to(rows[i][:, first + q : first + q + 1], shape) * spread[q]
            rows[i] = left
    return jnp.concatenate(rows, 0)


def products(scale, piece_refs, noise_ref, out_ref):
    scaled = jnp.concatenate([ref[...] for ref in piece_refs])
    members = scaled.shape[1]
    spread = scaled - jnp.sum(scaled, axis=1, keepdims=True) * (1.0 / members)
    misfit = noise_ref[...] - scale * scaled
    out_ref[:, :members] = product(spread, spread, 0, 0)
    out_ref[:, members:] = product(spread, misfit, 0, 0)


def update(scale, sums_ref, log_ref, updated_hbm, weights_ref, held_ref, sems):
    members = weights_ref.shape[0]
    half = members // 2
    diagonal = lax.broadcasted_iota(jnp.int32, (half, half), 0) == lax.broadcasted_iota(
        jnp.int32, (half, half), 1
    )
    shift = jnp.where(diagonal, inflation, 0.0)
    upper = product(inverse(sums_ref[:half, :half] + shift), sums_ref[:half, half:])
    lower = sums_ref[half:, half:] - product(sums_ref[half:, :half], upper)
    second = product(inverse(lower[:, :half] + shift), lower[:, half:])
    first = upper[:, half:] - product(upper[:, :half], second)
    mean = (
        jnp.sum(first, axis=0, keepdims=True) + jnp.sum(second, axis=0, keepdims=True)
    ) * (1.0 / members)
    weights_ref[:half] = (first - mean) * (1.0 / scale)
    weights_ref[half:] = (second - mean) * (1.0 / scale)
    chunk = log_ref.shape[0] // sems.shape[0]
    copies = []
    for n in range(sems.shape[0]):
        part = pl.ds(n * chunk, chunk)
        held_ref[part] = log_ref[part] + product(log_ref[part], weights_ref[...])
        copies.append(pltpu.make_async_copy(held_ref.at[part], updated_hbm.at[part], sems.at[n]))
        copies[-1].start()
    for copy in copies:
        copy.wait()


def smooth(scale, *refs):
    *piece_refs, noise_ref, log_ref, inner_ref, updated_hbm, final_hbm = refs[:-5]
    sums_ref, weights_ref, held_ref, sems, final_sem = refs[-5:]
    keep = pltpu.make_async_copy(inner_ref, final_hbm, final_sem)
    keep.start()
    products(scale, piece_refs, noise_ref, sums_ref)
    update(scale, sums_ref, log_ref, updated_hbm, weights_ref, held_ref, sems)
    keep.wait()


def finish(scale, sums_ref, log_ref, inner_ref, updated_hbm, final_hbm, *scratch):
    weights_ref, held_ref, sems, final_sem = scratch
    keep = pltpu.make_async_copy(inner_ref, final_hbm, final_sem)
    keep.start()
    update(scale, sums_ref, log_ref, updated_hbm, weights_ref, held_ref, sems)
    keep.wait()


def assimilate(scale, pieces, noise, log_rows, final, sums):
    members = noise.shape[1]
    pair = (members, 2 * members)
    outs = (f32(*log_rows.shape), f32(*final.shape))
    scratch = [
        pltpu.VMEM((members, members), jnp.float32),
        pltpu.VMEM(log_rows.shape, jnp.float32),
        pltpu.SemaphoreType.DMA((4,)),
        pltpu.SemaphoreType.DMA,
    ]
    if not sums:
        args = [*pieces, noise, log_rows, final]
        return call(
            functools.partial(smooth, scale), "smooth", outs, [VMEM] * len(args), args,
            scratch=[pltpu.VMEM(pair, jnp.float32), *scratch], flops=10**9,
            out_specs=(HBM, HBM),
        )
    args = [*pieces, noise]
    total = call(
        lambda *refs: products(scale, refs[:-2], *refs[-2:]), "products", f32(*pair),
        [VMEM] * len(args), args, flops=10**9,
    )
    for route in sums:
        total = total + send(total, route)
    args = [total, log_rows, final]
    return call(
        functools.partial(finish, scale), "finish", outs, [VMEM] * 3, args,
        scratch=scratch, flops=10**9, out_specs=(HBM, HBM),
    )


def shards(
    initial_thermal_state,
    logarithmic_diffusivity,
    rock_class_code,
    rock_class_diffusivity,
    advection_courant,
    probe_locations,
    observed_readings,
    probe_noise_deviation,
    random_starters,
):
    span_x, span_y, depth, members = initial_thermal_state.shape
    rows = (span_x, span_y)
    cells = span_x * span_y
    temperature = initial_thermal_state.reshape(cells, depth, members)
    log_cond = logarithmic_diffusivity.reshape(cells, depth, members)
    tile = f32(cells, depth, members)
    faces = [(span_y, depth, members)] * 2 + [(span_x, depth, members)] * 2
    levels = rock_class_diffusivity.shape
    columns = -(-cells // 128) * 128
    temperature, log_cond, outer, base, *sent = call(
        functools.partial(prepare, rows), "prepare",
        (tile, tile, tile, f32(depth, columns), *(f32(2, *face) for face in faces)),
        [HBM] * 4,
        [temperature, log_cond, rock_class_code, rock_class_diffusivity],
        scratch=[
            pltpu.VMEM((columns, 128), jnp.float32),
            pltpu.VMEM(rock_class_code.shape, jnp.int32),
            pltpu.SMEM(levels, jnp.float32),
            pltpu.SemaphoreType.DMA((4,)),
        ],
    )
    got = exchange(sent)
    half_cond, middle = call(
        functools.partial(middle_inside, rows), "middle_inside", (tile, tile),
        [SMEM] + [VMEM] * 4,
        [advection_courant, temperature, log_cond, base, outer],
        flops=10**7, aliases={4: 0},
    )
    middle, *sent = call(
        functools.partial(middle_border, rows), "middle_border",
        (tile, *(f32(*face) for face in faces)),
        [SMEM] + [VMEM] * 7,
        [advection_courant, temperature, half_cond, *got, middle],
        flops=10**7, aliases={7: 0},
    )
    got_middle = exchange(sent)
    final = call(
        functools.partial(final_inside, rows), "final_inside", tile,
        [SMEM] + [VMEM] * 2, [advection_courant, middle, half_cond], flops=10**7,
    )
    scale = (members - 1) ** 0.5
    obs_count = probe_locations.shape[0]
    final, scaled = call(
        functools.partial(observe, rows), "observe", (tile, f32(obs_count, members)),
        [SMEM] * 4 + [VMEM] * 11,
        [
            advection_courant, probe_locations, observed_readings,
            1.0 / (probe_noise_deviation * scale), middle, half_cond, *got_middle, *got, final,
        ],
        flops=10**7, aliases={14: 0},
    )
    count_x, count_y = lax.axis_size("gx"), lax.axis_size("gy")
    gathers, sums = plan_exchange(count_x, count_y, obs_count, 4 * members)
    pieces, owners = gather_blocks(scaled, gathers, count_x * count_y)
    owner = jnp.asarray(owners, jnp.int32)[lax.axis_index(("gx", "gy"))]
    obs_index = (
        owner[:, None] * obs_count + jnp.arange(obs_count, dtype=jnp.int32)[None, :]
    ).reshape(-1)
    noise = inflation**0.5 * perturbation(obs_index, random_starters)
    updated, final = assimilate(
        scale, pieces, noise, log_cond.reshape(-1, members), final, sums
    )
    shape = initial_thermal_state.shape
    return (final.reshape(shape), updated.reshape(shape))


def solution(mesh):
    placed = (
        P("gx", "gy", None, None),
        P("gx", "gy", None, None),
        P("gx", "gy", None),
        P(),
        P(),
        P(("gx", "gy")),
        P(("gx", "gy")),
        P(("gx", "gy")),
        P(),
    )
    return jax.shard_map(
        shards,
        mesh=mesh,
        in_specs=placed,
        out_specs=(P("gx", "gy", None, None), P("gx", "gy", None, None)),
        check_vma=False,
    )
```

```python
import functools

import jax
import jax.numpy as jnp
from jax import lax
from jax.experimental import pallas as pl
from jax.experimental.pallas import tpu as pltpu
from jax.sharding import PartitionSpec as P

inflation = 4.0
HIGHEST = lax.Precision.HIGHEST
UPDATE = lax.Precision.HIGH
VMEM = pl.BlockSpec(memory_space=pltpu.VMEM)
SMEM = pl.BlockSpec(memory_space=pltpu.SMEM)


HBM = pl.BlockSpec(memory_space=pltpu.HBM)


def f32(*shape):
    return jax.ShapeDtypeStruct(shape, jnp.float32)


def call(kernel, name, outs, specs, args, scratch=(), flops=0, out_specs=None, aliases={}):
    moved = sum(4 * a.size for a in args)
    return pl.pallas_call(
        kernel,
        out_shape=outs,
        in_specs=specs,
        out_specs=jax.tree.map(lambda _: VMEM, outs) if out_specs is None else out_specs,
        scratch_shapes=scratch,
        input_output_aliases=aliases,
        compiler_params=pltpu.CompilerParams(vmem_limit_bytes=20 << 20),
        cost_estimate=pl.CostEstimate(flops=flops, bytes_accessed=moved, transcendentals=0),
        name=name,
    )(*args)


def halo_routes(count_x, count_y):
    def flat(i, j):
        return i * count_y + j

    def turn(i, j):
        ahead = j + 1 if i % 2 == 0 else j - 1
        return (i, ahead) if 0 <= ahead < count_y else (i ^ 1, j)

    places = [(i, j) for i in range(count_x) for j in range(count_y)]
    right = [(flat(i, j), flat((i + 1) % count_x, j)) for i, j in places]
    along = [(flat(i, j), flat(*turn(i, j))) for i, j in places]
    return [right, back(right), along, back(along)]


def back(route):
    return [(b, a) for a, b in route]


def exchange(faces):
    routes = halo_routes(lax.axis_size("gx"), lax.axis_size("gy"))
    return [lax.ppermute(face, ("gx", "gy"), route) for face, route in zip(faces, routes)]


def border(rows, wanted):
    span_x, span_y = rows
    return [
        (x, y)
        for x in range(span_x)
        for y in range(span_y)
        if (x in (0, span_x - 1) or y in (0, span_y - 1)) == wanted
    ]


def is_even():
    return lax.rem(lax.axis_index("gx"), 2) == 0


def store_faces(field_ref, rows, put):
    span_x, span_y = rows
    even = is_even()
    for y in range(span_y):
        put(0, y, field_ref[(span_x - 1) * span_y + y])
        put(1, y, field_ref[y])
    for x in range(span_x):
        for route, at in (
            (2, jnp.where(even, span_y - 1, 0)),
            (3, jnp.where(even, 0, span_y - 1)),
        ):
            put(route, x, field_ref[x * span_y + at])


def conductivity(rows, cells, log_ref, columns_ref, h_ref):
    depth, members = log_ref.shape[1:]
    columns = columns_ref[...]
    for x, y in cells:
        cell = x * rows[1] + y
        base = jnp.broadcast_to(columns[:, cell : cell + 1], (depth, members))
        h_ref[cell] = base * jnp.exp(log_ref[cell])


def prepare(rows, t_hbm, log_hbm, code_hbm, rock_hbm, *rest):
    t_ref, log_ref, h_ref, columns_ref, *face_refs, turned, code_ref, rock_ref, sems = rest
    span_x, span_y = rows
    depth = t_ref.shape[1]
    copies = [
        pltpu.make_async_copy(source, target, sems.at[n])
        for n, (source, target) in enumerate(
            ((code_hbm, code_ref), (rock_hbm, rock_ref), (log_hbm, log_ref), (t_hbm, t_ref))
        )
    ]
    for copy in copies:
        copy.start()
    turned[...] = jnp.zeros_like(turned)
    copies[0].wait()
    copies[1].wait()
    for x in range(span_x):
        code = code_ref[x]
        base = jnp.zeros(code.shape, jnp.float32)
        for level in range(rock_ref.shape[0]):
            base = jnp.where(code == level, 0.5 * rock_ref[level], base)
        turned[x * span_y : (x + 1) * span_y, :depth] = base
    columns_ref[...] = jnp.transpose(turned[...])[:depth]
    copies[2].wait()
    conductivity(rows, border(rows, True), log_ref, columns_ref, h_ref)

    def put(field):
        def store(n, k, layer):
            face_refs[n][field, k] = layer

        return store

    store_faces(h_ref, rows, put(1))
    copies[3].wait()
    store_faces(t_ref, rows, put(0))


def advance(rows, cells, courant_ref, u_ref, h_ref, u_faces, h_faces, write):
    span_x, span_y = rows
    shape = u_ref.shape[1:]
    depth = shape[0]
    level = lax.broadcasted_iota(jnp.int32, shape, 0)
    courant = jnp.zeros(shape, jnp.float32)
    for z in range(depth):
        courant = jnp.where(level == z, courant_ref[z], courant)
    even = is_even()

    def beyond(faces, axis, after, k):
        name = ("gx", "gy")[axis]
        edge = lax.axis_index(name) == (lax.axis_size(name) - 1 if after else 0)
        if axis == 0:
            layer = faces(1 if after else 0, k)
        else:
            layer = jnp.where(even == after, faces(3, k), faces(2, k))
        return jnp.where(edge, 0.0, layer)

    def at(ref, faces, x, y):
        if x < 0 or x == span_x:
            return beyond(faces, 0, x > 0, y)
        if y < 0 or y == span_y:
            return beyond(faces, 1, y > 0, x)
        return ref[x * span_y + y]

    before, from_before = None, None
    for x, y in cells:
        u, h = u_ref[x * span_y + y], h_ref[x * span_y + y]

        def flow(i, j):
            step = at(u_ref, u_faces, i, j) - u
            return step, (h + at(h_ref, h_faces, i, j)) * step

        rise = jnp.where(level == depth - 1, 0.0, pltpu.roll(u, depth - 1, 0)) - u
        lift = (h + jnp.where(level == depth - 1, 0.0, pltpu.roll(h, depth - 1, 0))) * rise
        sink = jnp.where(level == 0, h * u, pltpu.roll(lift, 1, 0))
        west, from_west = flow(x - 1, y)
        from_east = flow(x + 1, y)[1]
        from_north = flow(x, y + 1)[1]
        from_south = from_before if before == (x, y - 1) else flow(x, y - 1)[1]
        before, from_before = (x, y), -from_north
        change = (from_east + from_west) + (from_north + from_south) + (lift - sink)
        write(x * span_y + y, u + change + courant * west)


def into(ref):
    def write(cell, value):
        ref[cell] = value

    return write


def middle_inside(rows, courant_ref, t_ref, log_ref, columns_ref, outer_ref, h_ref, middle_ref):
    del outer_ref
    inside = border(rows, False)
    conductivity(rows, inside, log_ref, columns_ref, h_ref)
    advance(rows, inside, courant_ref, t_ref, h_ref, None, None, into(middle_ref))


def middle_border(rows, courant_ref, t_ref, h_ref, *rest):
    got, middle_ref, face_refs = rest[:4], rest[5], rest[6:]
    advance(
        rows, border(rows, True), courant_ref, t_ref, h_ref,
        lambda n, k: got[n][0, k], lambda n, k: got[n][1, k], into(middle_ref),
    )

    def put(n, k, layer):
        face_refs[n][k] = layer

    store_faces(middle_ref, rows, put)


def final_inside(rows, courant_ref, u_ref, h_ref, final_ref):
    advance(rows, border(rows, False), courant_ref, u_ref, h_ref, None, None, into(final_ref))


def observe(rows, courant_ref, cells_ref, reading_ref, factor_ref, u_ref, h_ref, *rest):
    got_u, got_h, final_ref, scaled_ref = rest[:4], rest[4:8], rest[9], rest[10]
    depth = u_ref.shape[1]
    advance(
        rows, border(rows, True), courant_ref, u_ref, h_ref,
        lambda n, k: got_u[n][k], lambda n, k: got_h[n][1, k], into(final_ref),
    )
    for j in range(scaled_ref.shape[0]):
        cell = cells_ref[j]
        row = final_ref[lax.div(cell, depth), pl.ds(lax.rem(cell, depth), 1), :]
        scaled_ref[j : j + 1, :] = (row - reading_ref[j]) * factor_ref[j]


def modulo(value, divisor):
    quotient = (value.astype(jnp.float32) * (1.0 / divisor)).astype(jnp.int32)
    rest = value - quotient * divisor
    rest = jnp.where(rest < 0, rest + divisor, rest)
    return jnp.where(rest >= divisor, rest - divisor, rest)


def perturbation(obs_index, random_starters):
    first = random_starters * 7919 % 65521
    second = obs_index * 331 % 65521
    hashed = modulo(
        first[None, :] * (second[:, None] % 32749) + first[None, :] + second[:, None], 65521
    )
    uniform_value = (hashed.astype(jnp.float32) + 0.5) / 65521.0
    return jnp.sqrt(3.0) * (2.0 * uniform_value - 1.0)


def plan_exchange(count_x, count_y, rows, limit):
    def route(move):
        return [
            (i * count_y + j, a * count_y + b)
            for i in range(count_x)
            for j in range(count_y)
            for a, b in [move(i, j)]
        ]

    def shifted(axis, i, j, step):
        return (i ^ step, j) if axis == "gx" else (i, j ^ step)

    def across(axis, step):
        def move(i, j):
            at = i if axis == "gx" else j
            a, b = shifted(axis, i, j, step)
            return (a, b) if at < at ^ step else (a ^ 1, b)

        return route(move)

    def around(axis, low, high):
        def move(i, j):
            at = i if axis == "gx" else j
            step = low if bool(at & low) == bool(at & high) else high
            return shifted(axis, i, j, step)

        return route(move)

    gathers, sums = [], []
    for axis, count in (("gy", count_y), ("gx", count_x)):
        bits = [1 << b for b in range(count.bit_length() - 1)]
        while bits:
            if len(bits) > 1 and rows * 4 <= limit:
                high, low = bits.pop(), bits.pop()
                ring = around(axis, low, high)
                gathers.append([across(axis, low | high), ring, back(ring)])
                rows *= 4
                continue
            step = bits.pop()
            swap = route(functools.partial(shifted, axis, step=step))
            if rows * 2 <= limit:
                gathers.append([swap])
                rows *= 2
            else:
                sums.append(swap)
    return gathers, sums


def send(block, route):
    return lax.ppermute(block, ("gx", "gy"), route)


def pack(*refs):
    start = 0
    for ref in refs[:-1]:
        refs[-1][start : start + ref.shape[0], :] = ref[...]
        start += ref.shape[0]


def gather_blocks(block, gathers, devices):
    pieces, owners = [block], [[d] for d in range(devices)]
    for routes in gathers:
        if len(routes) > 1 and len(pieces) > 1:
            rows = sum(piece.shape[0] for piece in pieces)
            pieces = [
                call(pack, "pack", f32(rows, block.shape[1]), [VMEM] * len(pieces), pieces)
            ]
        pieces = pieces + [send(piece, route) for route in routes for piece in pieces]
        held = [list(own) for own in owners]
        for route in routes:
            for source, target in route:
                held[target] += owners[source]
        owners = held
    return pieces, owners


def product(a, b, over_a=1, over_b=0, precision=HIGHEST):
    return lax.dot_general(
        a, b, (((over_a,), (over_b,)), ((), ())), precision=precision,
        preferred_element_type=jnp.float32,
    )


def tree_sum(terms):
    while len(terms) > 1:
        terms = [sum(terms[n : n + 2]) for n in range(0, len(terms), 2)]
    return terms[0]


def factors(block):
    size, group = block.shape[0], 16
    shape = (group, size)
    lane = lax.broadcasted_iota(jnp.int32, shape, 1)
    sub = lax.broadcasted_iota(jnp.int32, shape, 0)
    count = size // group
    rows = [block[group * i : group * (i + 1), :] for i in range(count)]
    left, right = [], []

    def spread(values, at):
        return jnp.broadcast_to(values[:, at : at + 1], shape)

    for g in range(count):
        first = group * g
        inside = (lane >= first) & (lane < first + group)
        unit = jnp.where(lane - first == sub, 1.0, 0.0)
        columns = [spread(rows[g], first + q) for q in range(group)]
        held = jnp.where(inside, unit, rows[g])
        left.append(jnp.where(lane < first, rows[g], unit))
        for p in range(group):
            pivot = 1.0 / columns[p][p : p + 1, :]
            for q in range(p + 1, group):
                scaled = columns[q][p : p + 1, :] * pivot
                columns[q] = jnp.where(sub == p, scaled, columns[q] - columns[p] * scaled)
            scaled = held[p : p + 1, :] * pivot
            held = jnp.where(sub == p, scaled, held - columns[p] * scaled)
        right.append(jnp.where(lane < first + group, held, 0.0))
        for i in range(g + 1, count):
            rows[i] = jnp.where(inside, 0.0, rows[i]) - tree_sum(
                [spread(rows[i], first + q) * held[q : q + 1, :] for q in range(group)]
            )
    return jnp.concatenate(left), jnp.concatenate(right)


def products(scale, piece_refs, noise_ref):
    scaled = jnp.concatenate([ref[...] for ref in piece_refs])
    members = scaled.shape[1]
    spread = scaled - jnp.sum(scaled, axis=1, keepdims=True) * (1.0 / members)
    misfit = noise_ref[...] - scale * scaled
    return product(spread, jnp.concatenate([spread, misfit], axis=1), 0, 0)


def partial_products(scale, *refs):
    *piece_refs, noise_ref, sums_ref = refs
    sums_ref[...] = products(scale, piece_refs, noise_ref)


def update(scale, sums_ref, log_ref, updated_hbm, weights_ref, held_ref, sems):
    members = weights_ref.shape[0]
    half = members // 2
    diagonal = lax.broadcasted_iota(jnp.int32, (half, half), 0) == lax.broadcasted_iota(
        jnp.int32, (half, half), 1
    )
    shift = jnp.where(diagonal, inflation, 0.0)
    left, right = factors(sums_ref[:half, :half] + shift)
    both = product(jnp.concatenate([left, right]), sums_ref[:half, half:])
    upper = both[half:]
    lower = sums_ref[half:, half:] - product(both[:half, :half], upper, 0, 0)
    upper = product(left, upper, 0, 0)
    left, right = factors(lower[:, :half] + shift)
    second = product(product(left, right, 0, 0), lower[:, half:])
    first = upper[:, half:] - product(upper[:, :half], second)
    mean = (
        jnp.sum(first, axis=0, keepdims=True) + jnp.sum(second, axis=0, keepdims=True)
    ) * (1.0 / members)
    weights_ref[:half] = (first - mean) * (1.0 / scale)
    weights_ref[half:] = (second - mean) * (1.0 / scale)
    chunk = log_ref.shape[0] // sems.shape[0]
    copies = []
    for n in range(sems.shape[0]):
        part = pl.ds(n * chunk, chunk)
        held_ref[part] = log_ref[part] + product(
            log_ref[part], weights_ref[...], precision=UPDATE
        )
        copies.append(pltpu.make_async_copy(held_ref.at[part], updated_hbm.at[part], sems.at[n]))
        copies[-1].start()
    for copy in copies:
        copy.wait()


def smooth(scale, *refs):
    *piece_refs, noise_ref, near_ref, log_ref, inner_ref, updated_hbm, final_hbm = refs[:-5]
    sums_ref, weights_ref, held_ref, sems, final_sem = refs[-5:]
    keep = pltpu.make_async_copy(inner_ref, final_hbm, final_sem)
    keep.start()
    sums_ref[...] = near_ref[...] + products(scale, piece_refs, noise_ref)
    update(scale, sums_ref, log_ref, updated_hbm, weights_ref, held_ref, sems)
    keep.wait()


def finish(scale, sums_ref, log_ref, inner_ref, updated_hbm, final_hbm, *scratch):
    weights_ref, held_ref, sems, final_sem = scratch
    keep = pltpu.make_async_copy(inner_ref, final_hbm, final_sem)
    keep.start()
    update(scale, sums_ref, log_ref, updated_hbm, weights_ref, held_ref, sems)
    keep.wait()


def assimilate(scale, pieces, noise, log_rows, final, sums):
    members = log_rows.shape[1]
    pair = (members, 2 * members)
    outs = (f32(*log_rows.shape), f32(*final.shape))
    scratch = [
        pltpu.VMEM((members, members), jnp.float32),
        pltpu.VMEM(log_rows.shape, jnp.float32),
        pltpu.SemaphoreType.DMA((4,)),
        pltpu.SemaphoreType.DMA,
    ]
    def partial(blocks, noise_rows):
        args = [*blocks, noise_rows]
        return call(
            functools.partial(partial_products, scale), "partial_products", f32(*pair),
            [VMEM] * len(args), args, flops=10**8,
        )

    if not sums:
        near = len(pieces) // 2
        split = sum(piece.shape[0] for piece in pieces[:near])
        args = [
            *pieces[near:], noise[split:], partial(pieces[:near], noise[:split]), log_rows, final
        ]
        return call(
            functools.partial(smooth, scale), "smooth", outs, [VMEM] * len(args), args,
            scratch=[pltpu.VMEM(pair, jnp.float32), *scratch], flops=10**9,
            out_specs=(HBM, HBM),
        )
    total = partial(pieces, noise)
    for route in sums:
        total = total + send(total, route)
    args = [total, log_rows, final]
    return call(
        functools.partial(finish, scale), "finish", outs, [VMEM] * 3, args,
        scratch=scratch, flops=10**9, out_specs=(HBM, HBM),
    )


def shards(
    initial_thermal_state,
    logarithmic_diffusivity,
    rock_class_code,
    rock_class_diffusivity,
    advection_courant,
    probe_locations,
    observed_readings,
    probe_noise_deviation,
    random_starters,
):
    span_x, span_y, depth, members = initial_thermal_state.shape
    rows = (span_x, span_y)
    cells = span_x * span_y
    temperature = initial_thermal_state.reshape(cells, depth, members)
    log_cond = logarithmic_diffusivity.reshape(cells, depth, members)
    tile = f32(cells, depth, members)
    faces = [(span_y, depth, members)] * 2 + [(span_x, depth, members)] * 2
    levels = rock_class_diffusivity.shape
    columns = -(-cells // 128) * 128
    temperature, log_cond, outer, base, *sent = call(
        functools.partial(prepare, rows), "prepare",
        (tile, tile, tile, f32(depth, columns), *(f32(2, *face) for face in faces)),
        [HBM] * 4,
        [
            pltpu.with_memory_space_constraint(array, pltpu.HBM)
            for array in (temperature, log_cond, rock_class_code, rock_class_diffusivity)
        ],
        scratch=[
            pltpu.VMEM((columns, 128), jnp.float32),
            pltpu.VMEM(rock_class_code.shape, jnp.int32),
            pltpu.SMEM(levels, jnp.float32),
            pltpu.SemaphoreType.DMA((4,)),
        ],
    )
    got = exchange(sent)
    half_cond, middle = call(
        functools.partial(middle_inside, rows), "middle_inside", (tile, tile),
        [SMEM] + [VMEM] * 4,
        [advection_courant, temperature, log_cond, base, outer],
        flops=10**7, aliases={4: 0},
    )
    middle, *sent = call(
        functools.partial(middle_border, rows), "middle_border",
        (tile, *(f32(*face) for face in faces)),
        [SMEM] + [VMEM] * 7,
        [advection_courant, temperature, half_cond, *got, middle],
        flops=10**7, aliases={7: 0},
    )
    got_middle = exchange(sent)
    final = call(
        functools.partial(final_inside, rows), "final_inside", tile,
        [SMEM] + [VMEM] * 2, [advection_courant, middle, half_cond], flops=10**7,
    )
    scale = (members - 1) ** 0.5
    obs_count = probe_locations.shape[0]
    final, scaled = call(
        functools.partial(observe, rows), "observe", (tile, f32(obs_count, members)),
        [SMEM] * 4 + [VMEM] * 11,
        [
            advection_courant, probe_locations, observed_readings,
            1.0 / (probe_noise_deviation * scale), middle, half_cond, *got_middle, *got, final,
        ],
        flops=10**7, aliases={14: 0},
    )
    count_x, count_y = lax.axis_size("gx"), lax.axis_size("gy")
    gathers, sums = plan_exchange(count_x, count_y, obs_count, 4 * members)
    pieces, owners = gather_blocks(scaled, gathers, count_x * count_y)
    owner = jnp.asarray(owners, jnp.int32)[lax.axis_index(("gx", "gy"))]
    obs_index = (
        owner[:, None] * obs_count + jnp.arange(obs_count, dtype=jnp.int32)[None, :]
    ).reshape(-1)
    noise = inflation**0.5 * perturbation(obs_index, random_starters)
    updated, final = assimilate(
        scale, pieces, noise, log_cond.reshape(-1, members), final, sums
    )
    shape = initial_thermal_state.shape
    return (final.reshape(shape), updated.reshape(shape))


def solution(mesh):
    placed = (
        P("gx", "gy", None, None),
        P("gx", "gy", None, None),
        P("gx", "gy", None),
        P(),
        P(),
        P(("gx", "gy")),
        P(("gx", "gy")),
        P(("gx", "gy")),
        P(),
    )
    return jax.shard_map(
        shards,
        mesh=mesh,
        in_specs=placed,
        out_specs=(P("gx", "gy", None, None), P("gx", "gy", None, None)),
        check_vma=False,
    )
```

```python
import functools

import jax
import jax.numpy as jnp
from jax import lax
from jax.experimental import pallas as pl
from jax.experimental.pallas import tpu as pltpu
from jax.sharding import PartitionSpec as P

inflation = 4.0
HIGHEST = lax.Precision.HIGHEST
UPDATE = lax.Precision.HIGH
VMEM = pl.BlockSpec(memory_space=pltpu.VMEM)
SMEM = pl.BlockSpec(memory_space=pltpu.SMEM)


ORDER = (0, 2, 3, 1)
AT = (0, 3, 1, 2)
HBM = pl.BlockSpec(memory_space=pltpu.HBM)


def f32(*shape):
    return jax.ShapeDtypeStruct(shape, jnp.float32)


def call(kernel, name, outs, specs, args, scratch=(), flops=0, out_specs=None, aliases={}):
    moved = sum(4 * a.size for a in args)
    return pl.pallas_call(
        kernel,
        out_shape=outs,
        in_specs=specs,
        out_specs=jax.tree.map(lambda _: VMEM, outs) if out_specs is None else out_specs,
        scratch_shapes=scratch,
        input_output_aliases=aliases,
        compiler_params=pltpu.CompilerParams(vmem_limit_bytes=20 << 20),
        cost_estimate=pl.CostEstimate(flops=flops, bytes_accessed=moved, transcendentals=0),
        name=name,
    )(*args)


def halo_routes(count_x, count_y):
    def flat(i, j):
        return i * count_y + j

    def turn(i, j):
        ahead = j + 1 if i % 2 == 0 else j - 1
        return (i, ahead) if 0 <= ahead < count_y else (i ^ 1, j)

    places = [(i, j) for i in range(count_x) for j in range(count_y)]
    right = [(flat(i, j), flat((i + 1) % count_x, j)) for i, j in places]
    along = [(flat(i, j), flat(*turn(i, j))) for i, j in places]
    return [right, back(right), along, back(along)]


def back(route):
    return [(b, a) for a, b in route]


def exchange(faces):
    routes = halo_routes(lax.axis_size("gx"), lax.axis_size("gy"))
    return [lax.ppermute(face, ("gx", "gy"), route) for face, route in zip(faces, routes)]


def border(rows, wanted):
    span_x, span_y = rows
    return [
        (x, y)
        for x in range(span_x)
        for y in range(span_y)
        if (x in (0, span_x - 1) or y in (0, span_y - 1)) == wanted
    ]


def is_even():
    return lax.rem(lax.axis_index("gx"), 2) == 0


def store_faces(field_ref, rows, put):
    span_x, span_y = rows
    even = is_even()
    for y in range(span_y):
        put(0, y, field_ref[(span_x - 1) * span_y + y])
        put(1, y, field_ref[y])
    for x in range(span_x):
        for route, at in (
            (2, jnp.where(even, span_y - 1, 0)),
            (3, jnp.where(even, 0, span_y - 1)),
        ):
            put(route, x, field_ref[x * span_y + at])


def conductivity(rows, cells, log_ref, columns_ref, h_ref):
    depth, members = log_ref.shape[1:]
    columns = columns_ref[...]
    for x, y in cells:
        cell = x * rows[1] + y
        base = jnp.broadcast_to(columns[:, cell : cell + 1], (depth, members))
        h_ref[cell] = base * jnp.exp(log_ref[cell])


def prepare(rows, t_hbm, log_hbm, code_hbm, rock_hbm, *rest):
    t_ref, log_ref, columns_ref, *face_refs, h_ref, turned, code_ref, rock_ref, sems = rest
    span_x, span_y = rows
    depth = t_ref.shape[1]
    copies = [
        pltpu.make_async_copy(source, target, sems.at[n])
        for n, (source, target) in enumerate(
            ((code_hbm, code_ref), (rock_hbm, rock_ref), (log_hbm, log_ref), (t_hbm, t_ref))
        )
    ]
    for copy in copies:
        copy.start()
    turned[...] = jnp.zeros_like(turned)
    copies[0].wait()
    copies[1].wait()
    for x in range(span_x):
        code = code_ref[x]
        base = jnp.zeros(code.shape, jnp.float32)
        for level in range(rock_ref.shape[0]):
            base = jnp.where(code == level, 0.5 * rock_ref[level], base)
        turned[x * span_y : (x + 1) * span_y, :depth] = base
    columns_ref[...] = jnp.transpose(turned[...])[:depth]
    copies[2].wait()
    conductivity(rows, border(rows, True), log_ref, columns_ref, h_ref)

    def put(field):
        def store(n, k, layer):
            face_refs[n][field, k] = layer

        return store

    store_faces(h_ref, rows, put(1))
    copies[3].wait()
    store_faces(t_ref, rows, put(0))


def advance(rows, cells, courant_ref, u_ref, h_ref, u_faces, h_faces, write):
    span_x, span_y = rows
    shape = u_ref.shape[1:]
    depth = shape[0]
    level = lax.broadcasted_iota(jnp.int32, shape, 0)
    courant = jnp.zeros(shape, jnp.float32)
    for z in range(depth):
        courant = jnp.where(level == z, courant_ref[z], courant)
    even = is_even()

    def beyond(faces, axis, after, k):
        name = ("gx", "gy")[axis]
        edge = lax.axis_index(name) == (lax.axis_size(name) - 1 if after else 0)
        if axis == 0:
            layer = faces(1 if after else 0, k)
        else:
            layer = jnp.where(even == after, faces(3, k), faces(2, k))
        return jnp.where(edge, 0.0, layer)

    def at(ref, faces, x, y):
        if x < 0 or x == span_x:
            return beyond(faces, 0, x > 0, y)
        if y < 0 or y == span_y:
            return beyond(faces, 1, y > 0, x)
        return ref[x * span_y + y]

    before, from_before = None, None
    for x, y in cells:
        u, h = u_ref[x * span_y + y], h_ref[x * span_y + y]

        def flow(i, j):
            step = at(u_ref, u_faces, i, j) - u
            return step, (h + at(h_ref, h_faces, i, j)) * step

        rise = jnp.where(level == depth - 1, 0.0, pltpu.roll(u, depth - 1, 0)) - u
        lift = (h + jnp.where(level == depth - 1, 0.0, pltpu.roll(h, depth - 1, 0))) * rise
        sink = jnp.where(level == 0, h * u, pltpu.roll(lift, 1, 0))
        west, from_west = flow(x - 1, y)
        from_east = flow(x + 1, y)[1]
        from_north = flow(x, y + 1)[1]
        from_south = from_before if before == (x, y - 1) else flow(x, y - 1)[1]
        before, from_before = (x, y), -from_north
        change = (from_east + from_west) + (from_north + from_south) + (lift - sink)
        write(x * span_y + y, u + change + courant * west)


def into(ref):
    def write(cell, value):
        ref[cell] = value

    return write


def middle_inside(rows, courant_ref, t_ref, log_ref, columns_ref, h_ref, middle_ref):
    inside = border(rows, False)
    conductivity(rows, border(rows, True) + inside, log_ref, columns_ref, h_ref)
    advance(rows, inside, courant_ref, t_ref, h_ref, None, None, into(middle_ref))


def middle_border(rows, courant_ref, t_ref, h_ref, *rest):
    got, middle_ref, face_refs = rest[:4], rest[5], rest[6:]
    advance(
        rows, border(rows, True), courant_ref, t_ref, h_ref,
        lambda n, k: got[AT[n]][0, k], lambda n, k: got[AT[n]][1, k], into(middle_ref),
    )

    def put(n, k, layer):
        face_refs[n][k] = layer

    store_faces(middle_ref, rows, put)


def final_inside(rows, courant_ref, u_ref, h_ref, final_ref):
    advance(rows, border(rows, False), courant_ref, u_ref, h_ref, None, None, into(final_ref))


def observe(rows, courant_ref, cells_ref, reading_ref, factor_ref, u_ref, h_ref, *rest):
    got_u, got_h, final_ref, scaled_ref = rest[:4], rest[4:8], rest[9], rest[10]
    depth = u_ref.shape[1]
    advance(
        rows, border(rows, True), courant_ref, u_ref, h_ref,
        lambda n, k: got_u[AT[n]][k], lambda n, k: got_h[AT[n]][1, k], into(final_ref),
    )
    for j in range(scaled_ref.shape[0]):
        cell = cells_ref[j]
        row = final_ref[lax.div(cell, depth), pl.ds(lax.rem(cell, depth), 1), :]
        scaled_ref[j : j + 1, :] = (row - reading_ref[j]) * factor_ref[j]


def modulo(value, divisor):
    quotient = (value.astype(jnp.float32) * (1.0 / divisor)).astype(jnp.int32)
    rest = value - quotient * divisor
    rest = jnp.where(rest < 0, rest + divisor, rest)
    return jnp.where(rest >= divisor, rest - divisor, rest)


def perturbation(obs_index, random_starters):
    first = random_starters * 7919 % 65521
    second = obs_index * 331 % 65521
    hashed = modulo(
        first[None, :] * (second[:, None] % 32749) + first[None, :] + second[:, None], 65521
    )
    uniform_value = (hashed.astype(jnp.float32) + 0.5) / 65521.0
    return jnp.sqrt(3.0) * (2.0 * uniform_value - 1.0)


def plan_exchange(count_x, count_y, rows, limit):
    def route(move):
        return [
            (i * count_y + j, a * count_y + b)
            for i in range(count_x)
            for j in range(count_y)
            for a, b in [move(i, j)]
        ]

    def shifted(axis, i, j, step):
        return (i ^ step, j) if axis == "gx" else (i, j ^ step)

    def across(axis, step):
        def move(i, j):
            at = i if axis == "gx" else j
            a, b = shifted(axis, i, j, step)
            return (a, b) if at < at ^ step else (a ^ 1, b)

        return route(move)

    def around(axis, low, high):
        def move(i, j):
            at = i if axis == "gx" else j
            step = low if bool(at & low) == bool(at & high) else high
            return shifted(axis, i, j, step)

        return route(move)

    gathers, sums = [], []
    for axis, count in (("gy", count_y), ("gx", count_x)):
        bits = [1 << b for b in range(count.bit_length() - 1)]
        while bits:
            if len(bits) > 1 and rows * 4 <= limit:
                high, low = bits.pop(), bits.pop()
                ring = around(axis, low, high)
                gathers.append([ring, back(ring), across(axis, low | high)])
                rows *= 4
                continue
            step = bits.pop()
            swap = route(functools.partial(shifted, axis, step=step))
            if rows * 2 <= limit:
                gathers.append([swap])
                rows *= 2
            else:
                sums.append(swap)
    return gathers, sums


def send(block, route):
    return lax.ppermute(block, ("gx", "gy"), route)


def pack(*refs):
    start = 0
    for ref in refs[:-1]:
        refs[-1][start : start + ref.shape[0], :] = ref[...]
        start += ref.shape[0]


def gather_blocks(block, gathers, devices):
    pieces, owners = [block], [[d] for d in range(devices)]
    for routes in gathers:
        if len(routes) > 1 and len(pieces) > 1:
            rows = sum(piece.shape[0] for piece in pieces)
            pieces = [
                call(pack, "pack", f32(rows, block.shape[1]), [VMEM] * len(pieces), pieces)
            ]
        pieces = pieces + [send(piece, route) for route in routes for piece in pieces]
        held = [list(own) for own in owners]
        for route in routes:
            for source, target in route:
                held[target] += owners[source]
        owners = held
    return pieces, owners


def product(a, b, over_a=1, over_b=0, precision=HIGHEST):
    return lax.dot_general(
        a, b, (((over_a,), (over_b,)), ((), ())), precision=precision,
        preferred_element_type=jnp.float32,
    )


def tree_sum(terms):
    while len(terms) > 1:
        terms = [sum(terms[n : n + 2]) for n in range(0, len(terms), 2)]
    return terms[0]


def factors(block):
    size, group = block.shape[0], 16
    shape = (group, size)
    lane = lax.broadcasted_iota(jnp.int32, shape, 1)
    sub = lax.broadcasted_iota(jnp.int32, shape, 0)
    count = size // group
    rows = [block[group * i : group * (i + 1), :] for i in range(count)]
    left, right = [], []

    def spread(values, at):
        return jnp.broadcast_to(values[:, at : at + 1], shape)

    for g in range(count):
        first = group * g
        inside = (lane >= first) & (lane < first + group)
        unit = jnp.where(lane - first == sub, 1.0, 0.0)
        columns = [spread(rows[g], first + q) for q in range(group)]
        held = jnp.where(inside, unit, rows[g])
        left.append(jnp.where(lane < first, rows[g], unit))
        for p in range(group):
            pivot = 1.0 / columns[p][p : p + 1, :]
            for q in range(p + 1, group):
                scaled = columns[q][p : p + 1, :] * pivot
                columns[q] = jnp.where(sub == p, scaled, columns[q] - columns[p] * scaled)
            scaled = held[p : p + 1, :] * pivot
            held = jnp.where(sub == p, scaled, held - columns[p] * scaled)
        right.append(jnp.where(lane < first + group, held, 0.0))
        for i in range(g + 1, count):
            rows[i] = jnp.where(inside, 0.0, rows[i]) - tree_sum(
                [spread(rows[i], first + q) * held[q : q + 1, :] for q in range(group)]
            )
    return jnp.concatenate(left), jnp.concatenate(right)


def products(scale, piece_refs, noise_ref):
    scaled = jnp.concatenate([ref[...] for ref in piece_refs])
    members = scaled.shape[1]
    spread = scaled - jnp.sum(scaled, axis=1, keepdims=True) * (1.0 / members)
    misfit = noise_ref[...] - scale * scaled
    return product(spread, jnp.concatenate([spread, misfit], axis=1), 0, 0)


def partial_products(scale, *refs):
    *piece_refs, noise_ref, sums_ref = refs
    sums_ref[...] = products(scale, piece_refs, noise_ref)


def update(scale, sums_ref, log_ref, updated_hbm, weights_ref, held_ref, sems):
    members = weights_ref.shape[0]
    half = members // 2
    diagonal = lax.broadcasted_iota(jnp.int32, (half, half), 0) == lax.broadcasted_iota(
        jnp.int32, (half, half), 1
    )
    shift = jnp.where(diagonal, inflation, 0.0)
    left, right = factors(sums_ref[:half, :half] + shift)
    both = product(jnp.concatenate([left, right]), sums_ref[:half, half:])
    upper = both[half:]
    lower = sums_ref[half:, half:] - product(both[:half, :half], upper, 0, 0)
    upper = product(left, upper, 0, 0)
    left, right = factors(lower[:, :half] + shift)
    second = product(product(left, right, 0, 0), lower[:, half:])
    first = upper[:, half:] - product(upper[:, :half], second)
    mean = (
        jnp.sum(first, axis=0, keepdims=True) + jnp.sum(second, axis=0, keepdims=True)
    ) * (1.0 / members)
    weights_ref[:half] = (first - mean) * (1.0 / scale)
    weights_ref[half:] = (second - mean) * (1.0 / scale)
    chunk = log_ref.shape[0] // sems.shape[0]
    copies = []
    for n in range(sems.shape[0]):
        part = pl.ds(n * chunk, chunk)
        held_ref[part] = log_ref[part] + product(
            log_ref[part], weights_ref[...], precision=UPDATE
        )
        copies.append(pltpu.make_async_copy(held_ref.at[part], updated_hbm.at[part], sems.at[n]))
        copies[-1].start()
    for copy in copies:
        copy.wait()


def smooth(scale, *refs):
    *piece_refs, noise_ref, near_ref, log_ref, inner_ref, updated_hbm, final_hbm = refs[:-5]
    sums_ref, weights_ref, held_ref, sems, final_sem = refs[-5:]
    keep = pltpu.make_async_copy(inner_ref, final_hbm, final_sem)
    keep.start()
    sums_ref[...] = near_ref[...] + products(scale, piece_refs, noise_ref)
    update(scale, sums_ref, log_ref, updated_hbm, weights_ref, held_ref, sems)
    keep.wait()


def finish(scale, sums_ref, log_ref, inner_ref, updated_hbm, final_hbm, *scratch):
    weights_ref, held_ref, sems, final_sem = scratch
    keep = pltpu.make_async_copy(inner_ref, final_hbm, final_sem)
    keep.start()
    update(scale, sums_ref, log_ref, updated_hbm, weights_ref, held_ref, sems)
    keep.wait()


def assimilate(scale, pieces, noise, log_rows, final, sums):
    members = log_rows.shape[1]
    pair = (members, 2 * members)
    outs = (f32(*log_rows.shape), f32(*final.shape))
    scratch = [
        pltpu.VMEM((members, members), jnp.float32),
        pltpu.VMEM(log_rows.shape, jnp.float32),
        pltpu.SemaphoreType.DMA((4,)),
        pltpu.SemaphoreType.DMA,
    ]
    def partial(blocks, noise_rows):
        args = [*blocks, noise_rows]
        return call(
            functools.partial(partial_products, scale), "partial_products", f32(*pair),
            [VMEM] * len(args), args, flops=10**8,
        )

    if not sums:
        near = len(pieces) // 2
        split = sum(piece.shape[0] for piece in pieces[:near])
        args = [
            *pieces[near:], noise[split:], partial(pieces[:near], noise[:split]), log_rows, final
        ]
        return call(
            functools.partial(smooth, scale), "smooth", outs, [VMEM] * len(args), args,
            scratch=[pltpu.VMEM(pair, jnp.float32), *scratch], flops=10**9,
            out_specs=(HBM, HBM),
        )
    total = partial(pieces, noise)
    for route in sums:
        total = total + send(total, route)
    args = [total, log_rows, final]
    return call(
        functools.partial(finish, scale), "finish", outs, [VMEM] * 3, args,
        scratch=scratch, flops=10**9, out_specs=(HBM, HBM),
    )


def shards(
    initial_thermal_state,
    logarithmic_diffusivity,
    rock_class_code,
    rock_class_diffusivity,
    advection_courant,
    probe_locations,
    observed_readings,
    probe_noise_deviation,
    random_starters,
):
    span_x, span_y, depth, members = initial_thermal_state.shape
    rows = (span_x, span_y)
    cells = span_x * span_y
    temperature = initial_thermal_state.reshape(cells, depth, members)
    log_cond = logarithmic_diffusivity.reshape(cells, depth, members)
    tile = f32(cells, depth, members)
    faces = [(span_y, depth, members)] * 2 + [(span_x, depth, members)] * 2
    levels = rock_class_diffusivity.shape
    columns = -(-cells // 128) * 128
    temperature, log_cond, base, *sent = call(
        functools.partial(prepare, rows), "prepare",
        (tile, tile, f32(depth, columns), *(f32(2, *face) for face in faces)),
        [HBM] * 4,
        [
            pltpu.with_memory_space_constraint(array, pltpu.HBM)
            for array in (temperature, log_cond, rock_class_code, rock_class_diffusivity)
        ],
        scratch=[
            pltpu.VMEM((cells, depth, members), jnp.float32),
            pltpu.VMEM((columns, 128), jnp.float32),
            pltpu.VMEM(rock_class_code.shape, jnp.int32),
            pltpu.SMEM(levels, jnp.float32),
            pltpu.SemaphoreType.DMA((4,)),
        ],
    )
    got = exchange(sent)
    half_cond, middle = call(
        functools.partial(middle_inside, rows), "middle_inside", (tile, tile),
        [SMEM] + [VMEM] * 3, [advection_courant, temperature, log_cond, base],
        flops=10**7,
    )
    middle, *sent = call(
        functools.partial(middle_border, rows), "middle_border",
        (tile, *(f32(*face) for face in faces)),
        [SMEM] + [VMEM] * 7,
        [advection_courant, temperature, half_cond, *[got[n] for n in ORDER], middle],
        flops=10**7, aliases={7: 0},
    )
    got_middle = exchange(sent)
    final = call(
        functools.partial(final_inside, rows), "final_inside", tile,
        [SMEM] + [VMEM] * 2, [advection_courant, middle, half_cond], flops=10**7,
    )
    scale = (members - 1) ** 0.5
    obs_count = probe_locations.shape[0]
    final, scaled = call(
        functools.partial(observe, rows), "observe", (tile, f32(obs_count, members)),
        [SMEM] * 4 + [VMEM] * 11,
        [
            advection_courant, probe_locations, observed_readings,
            1.0 / (probe_noise_deviation * scale), middle, half_cond, *[got_middle[n] for n in ORDER], *[got[n] for n in ORDER], final,
        ],
        flops=10**7, aliases={14: 0},
    )
    count_x, count_y = lax.axis_size("gx"), lax.axis_size("gy")
    gathers, sums = plan_exchange(count_x, count_y, obs_count, 4 * members)
    pieces, owners = gather_blocks(scaled, gathers, count_x * count_y)
    owner = jnp.asarray(owners, jnp.int32)[lax.axis_index(("gx", "gy"))]
    obs_index = (
        owner[:, None] * obs_count + jnp.arange(obs_count, dtype=jnp.int32)[None, :]
    ).reshape(-1)
    noise = inflation**0.5 * perturbation(obs_index, random_starters)
    updated, final = assimilate(
        scale, pieces, noise, log_cond.reshape(-1, members), final, sums
    )
    shape = initial_thermal_state.shape
    return (final.reshape(shape), updated.reshape(shape))


def solution(mesh):
    placed = (
        P("gx", "gy", None, None),
        P("gx", "gy", None, None),
        P("gx", "gy", None),
        P(),
        P(),
        P(("gx", "gy")),
        P(("gx", "gy")),
        P(("gx", "gy")),
        P(),
    )
    return jax.shard_map(
        shards,
        mesh=mesh,
        in_specs=placed,
        out_specs=(P("gx", "gy", None, None), P("gx", "gy", None, None)),
        check_vma=False,
    )
```

```python
import functools

import jax
import jax.numpy as jnp
from jax import lax
from jax.experimental import pallas as pl
from jax.experimental.pallas import tpu as pltpu
from jax.sharding import PartitionSpec as P

inflation = 4.0
HIGHEST = lax.Precision.HIGHEST
THREE_PASS = lax.Precision.HIGH
VMEM = pl.BlockSpec(memory_space=pltpu.VMEM)
SMEM = pl.BlockSpec(memory_space=pltpu.SMEM)


ORDER = (0, 2, 3, 1)
AT = (0, 3, 1, 2)
HBM = pl.BlockSpec(memory_space=pltpu.HBM)


def f32(*shape):
    return jax.ShapeDtypeStruct(shape, jnp.float32)


def call(kernel, name, outs, specs, args, scratch=(), flops=0, out_specs=None, aliases={}):
    moved = sum(4 * a.size for a in args)
    return pl.pallas_call(
        kernel,
        out_shape=outs,
        in_specs=specs,
        out_specs=jax.tree.map(lambda _: VMEM, outs) if out_specs is None else out_specs,
        scratch_shapes=scratch,
        input_output_aliases=aliases,
        compiler_params=pltpu.CompilerParams(vmem_limit_bytes=20 << 20),
        cost_estimate=pl.CostEstimate(flops=flops, bytes_accessed=moved, transcendentals=0),
        name=name,
    )(*args)


def halo_routes(count_x, count_y):
    def flat(i, j):
        return i * count_y + j

    def turn(i, j):
        ahead = j + 1 if i % 2 == 0 else j - 1
        return (i, ahead) if 0 <= ahead < count_y else (i ^ 1, j)

    places = [(i, j) for i in range(count_x) for j in range(count_y)]
    right = [(flat(i, j), flat((i + 1) % count_x, j)) for i, j in places]
    along = [(flat(i, j), flat(*turn(i, j))) for i, j in places]
    return [right, back(right), along, back(along)]


def back(route):
    return [(b, a) for a, b in route]


def exchange(faces):
    routes = halo_routes(lax.axis_size("gx"), lax.axis_size("gy"))
    return [lax.ppermute(face, ("gx", "gy"), route) for face, route in zip(faces, routes)]


def border(rows, wanted):
    span_x, span_y = rows
    return [
        (x, y)
        for x in range(span_x)
        for y in range(span_y)
        if (x in (0, span_x - 1) or y in (0, span_y - 1)) == wanted
    ]


def is_even():
    return lax.rem(lax.axis_index("gx"), 2) == 0


def store_faces(field_ref, rows, put):
    span_x, span_y = rows
    even = is_even()
    for y in range(span_y):
        put(0, y, field_ref[(span_x - 1) * span_y + y])
        put(1, y, field_ref[y])
    for x in range(span_x):
        for route, at in (
            (2, jnp.where(even, span_y - 1, 0)),
            (3, jnp.where(even, 0, span_y - 1)),
        ):
            put(route, x, field_ref[x * span_y + at])


def conductivity(rows, cells, log_ref, columns_ref, h_ref):
    depth, members = log_ref.shape[1:]
    columns = columns_ref[...]
    for x, y in cells:
        cell = x * rows[1] + y
        base = jnp.broadcast_to(columns[:, cell : cell + 1], (depth, members))
        h_ref[cell] = base * jnp.exp(log_ref[cell])


def prepare(rows, t_hbm, log_hbm, code_hbm, rock_hbm, *rest):
    t_ref, log_ref, columns_ref, *face_refs, h_ref, turned, code_ref, rock_ref, sems = rest
    span_x, span_y = rows
    depth = t_ref.shape[1]
    copies = [
        pltpu.make_async_copy(source, target, sems.at[n])
        for n, (source, target) in enumerate(
            ((code_hbm, code_ref), (rock_hbm, rock_ref), (log_hbm, log_ref), (t_hbm, t_ref))
        )
    ]
    for copy in copies:
        copy.start()
    turned[...] = jnp.zeros_like(turned)
    copies[0].wait()
    copies[1].wait()
    for x in range(span_x):
        code = code_ref[x]
        base = jnp.zeros(code.shape, jnp.float32)
        for level in range(rock_ref.shape[0]):
            base = jnp.where(code == level, 0.5 * rock_ref[level], base)
        turned[x * span_y : (x + 1) * span_y, :depth] = base
    columns_ref[...] = jnp.transpose(turned[...])[:depth]
    copies[2].wait()
    conductivity(rows, border(rows, True), log_ref, columns_ref, h_ref)

    def put(field):
        def store(n, k, layer):
            face_refs[n][field, k] = layer

        return store

    store_faces(h_ref, rows, put(1))
    copies[3].wait()
    store_faces(t_ref, rows, put(0))


def advance(rows, cells, courant_ref, u_ref, h_ref, u_faces, h_faces, write):
    span_x, span_y = rows
    shape = u_ref.shape[1:]
    depth = shape[0]
    level = lax.broadcasted_iota(jnp.int32, shape, 0)
    courant = jnp.zeros(shape, jnp.float32)
    for z in range(depth):
        courant = jnp.where(level == z, courant_ref[z], courant)
    even = is_even()

    def beyond(faces, axis, after, k):
        name = ("gx", "gy")[axis]
        edge = lax.axis_index(name) == (lax.axis_size(name) - 1 if after else 0)
        if axis == 0:
            layer = faces(1 if after else 0, k)
        else:
            layer = jnp.where(even == after, faces(3, k), faces(2, k))
        return jnp.where(edge, 0.0, layer)

    def at(ref, faces, x, y):
        if x < 0 or x == span_x:
            return beyond(faces, 0, x > 0, y)
        if y < 0 or y == span_y:
            return beyond(faces, 1, y > 0, x)
        return ref[x * span_y + y]

    before, from_before = None, None
    for x, y in cells:
        u, h = u_ref[x * span_y + y], h_ref[x * span_y + y]

        def flow(i, j):
            step = at(u_ref, u_faces, i, j) - u
            return step, (h + at(h_ref, h_faces, i, j)) * step

        rise = jnp.where(level == depth - 1, 0.0, pltpu.roll(u, depth - 1, 0)) - u
        lift = (h + jnp.where(level == depth - 1, 0.0, pltpu.roll(h, depth - 1, 0))) * rise
        sink = jnp.where(level == 0, h * u, pltpu.roll(lift, 1, 0))
        west, from_west = flow(x - 1, y)
        from_east = flow(x + 1, y)[1]
        from_north = flow(x, y + 1)[1]
        from_south = from_before if before == (x, y - 1) else flow(x, y - 1)[1]
        before, from_before = (x, y), -from_north
        change = (from_east + from_west) + (from_north + from_south) + (lift - sink)
        write(x * span_y + y, u + change + courant * west)


def into(ref):
    def write(cell, value):
        ref[cell] = value

    return write


def middle_inside(rows, courant_ref, t_ref, log_ref, columns_ref, h_ref, middle_ref):
    inside = border(rows, False)
    conductivity(rows, border(rows, True) + inside, log_ref, columns_ref, h_ref)
    advance(rows, inside, courant_ref, t_ref, h_ref, None, None, into(middle_ref))


def middle_border(rows, courant_ref, t_ref, h_ref, *rest):
    got, middle_ref, face_refs = rest[:4], rest[5], rest[6:]
    advance(
        rows, border(rows, True), courant_ref, t_ref, h_ref,
        lambda n, k: got[AT[n]][0, k], lambda n, k: got[AT[n]][1, k], into(middle_ref),
    )

    def put(n, k, layer):
        face_refs[n][k] = layer

    store_faces(middle_ref, rows, put)


def final_inside(rows, courant_ref, u_ref, h_ref, final_ref):
    advance(rows, border(rows, False), courant_ref, u_ref, h_ref, None, None, into(final_ref))


def observe(rows, courant_ref, cells_ref, reading_ref, factor_ref, u_ref, h_ref, *rest):
    got_u, got_h, final_ref, scaled_ref = rest[:4], rest[4:8], rest[9], rest[10]
    depth = u_ref.shape[1]
    advance(
        rows, border(rows, True), courant_ref, u_ref, h_ref,
        lambda n, k: got_u[AT[n]][k], lambda n, k: got_h[AT[n]][1, k], into(final_ref),
    )
    for j in range(scaled_ref.shape[0]):
        cell = cells_ref[j]
        row = final_ref[lax.div(cell, depth), pl.ds(lax.rem(cell, depth), 1), :]
        scaled_ref[j : j + 1, :] = (row - reading_ref[j]) * factor_ref[j]


def modulo(value, divisor):
    quotient = (value.astype(jnp.float32) * (1.0 / divisor)).astype(jnp.int32)
    rest = value - quotient * divisor
    rest = jnp.where(rest < 0, rest + divisor, rest)
    return jnp.where(rest >= divisor, rest - divisor, rest)


def perturbation(obs_index, random_starters):
    first = random_starters * 7919 % 65521
    second = obs_index * 331 % 65521
    hashed = modulo(
        first[None, :] * (second[:, None] % 32749) + first[None, :] + second[:, None], 65521
    )
    uniform_value = (hashed.astype(jnp.float32) + 0.5) / 65521.0
    return jnp.sqrt(3.0) * (2.0 * uniform_value - 1.0)


def plan_exchange(count_x, count_y, rows, limit):
    def route(move):
        return [
            (i * count_y + j, a * count_y + b)
            for i in range(count_x)
            for j in range(count_y)
            for a, b in [move(i, j)]
        ]

    def shifted(axis, i, j, step):
        return (i ^ step, j) if axis == "gx" else (i, j ^ step)

    def across(axis, step):
        def move(i, j):
            at = i if axis == "gx" else j
            a, b = shifted(axis, i, j, step)
            return (a, b) if at < at ^ step else (a ^ 1, b)

        return route(move)

    def around(axis, low, high):
        def move(i, j):
            at = i if axis == "gx" else j
            step = low if bool(at & low) == bool(at & high) else high
            return shifted(axis, i, j, step)

        return route(move)

    gathers, sums = [], []
    for axis, count in (("gy", count_y), ("gx", count_x)):
        bits = [1 << b for b in range(count.bit_length() - 1)]
        while bits:
            if len(bits) > 1 and rows * 4 <= limit:
                high, low = bits.pop(), bits.pop()
                ring = around(axis, low, high)
                gathers.append([ring, back(ring), across(axis, low | high)])
                rows *= 4
                continue
            step = bits.pop()
            swap = route(functools.partial(shifted, axis, step=step))
            if rows * 2 <= limit:
                gathers.append([swap])
                rows *= 2
            else:
                sums.append(swap)
    return gathers, sums


def send(block, route):
    return lax.ppermute(block, ("gx", "gy"), route)


def pack(*refs):
    start = 0
    for ref in refs[:-1]:
        refs[-1][start : start + ref.shape[0], :] = ref[...]
        start += ref.shape[0]


def gather_blocks(block, gathers, devices):
    pieces, owners = [block], [[d] for d in range(devices)]
    for routes in gathers:
        if len(routes) > 1 and len(pieces) > 1:
            rows = sum(piece.shape[0] for piece in pieces)
            pieces = [
                call(pack, "pack", f32(rows, block.shape[1]), [VMEM] * len(pieces), pieces)
            ]
        pieces = pieces + [send(piece, route) for route in routes for piece in pieces]
        held = [list(own) for own in owners]
        for route in routes:
            for source, target in route:
                held[target] += owners[source]
        owners = held
    return pieces, owners


def product(a, b, over_a=1, over_b=0, precision=HIGHEST):
    return lax.dot_general(
        a, b, (((over_a,), (over_b,)), ((), ())), precision=precision,
        preferred_element_type=jnp.float32,
    )


def tree_sum(terms):
    while len(terms) > 1:
        terms = [sum(terms[n : n + 2]) for n in range(0, len(terms), 2)]
    return terms[0]


def factors(block):
    size, group = block.shape[0], 16
    shape = (group, size)
    lane = lax.broadcasted_iota(jnp.int32, shape, 1)
    sub = lax.broadcasted_iota(jnp.int32, shape, 0)
    count = size // group
    rows = [block[group * i : group * (i + 1), :] for i in range(count)]
    left, right = [], []

    def spread(values, at):
        return jnp.broadcast_to(values[:, at : at + 1], shape)

    for g in range(count):
        first = group * g
        inside = (lane >= first) & (lane < first + group)
        unit = jnp.where(lane - first == sub, 1.0, 0.0)
        columns = [spread(rows[g], first + q) for q in range(group)]
        held = jnp.where(inside, unit, rows[g])
        left.append(jnp.where(lane < first, rows[g], unit))
        for p in range(group):
            pivot = 1.0 / columns[p][p : p + 1, :]
            for q in range(p + 1, group):
                scaled = columns[q][p : p + 1, :] * pivot
                columns[q] = jnp.where(sub == p, scaled, columns[q] - columns[p] * scaled)
            scaled = held[p : p + 1, :] * pivot
            held = jnp.where(sub == p, scaled, held - columns[p] * scaled)
        right.append(jnp.where(lane < first + group, held, 0.0))
        for i in range(g + 1, count):
            rows[i] = jnp.where(inside, 0.0, rows[i]) - tree_sum(
                [spread(rows[i], first + q) * held[q : q + 1, :] for q in range(group)]
            )
    return jnp.concatenate(left), jnp.concatenate(right)


def products(scale, piece_refs, noise_ref):
    scaled = jnp.concatenate([ref[...] for ref in piece_refs])
    members = scaled.shape[1]
    spread = scaled - jnp.sum(scaled, axis=1, keepdims=True) * (1.0 / members)
    misfit = noise_ref[...] - scale * scaled
    return product(spread, jnp.concatenate([spread, misfit], axis=1), 0, 0, THREE_PASS)


def partial_products(scale, *refs):
    *piece_refs, noise_ref, sums_ref = refs
    sums_ref[...] = products(scale, piece_refs, noise_ref)


def update(scale, sums_ref, log_ref, updated_hbm, weights_ref, held_ref, sems):
    members = weights_ref.shape[0]
    half = members // 2
    diagonal = lax.broadcasted_iota(jnp.int32, (half, half), 0) == lax.broadcasted_iota(
        jnp.int32, (half, half), 1
    )
    shift = jnp.where(diagonal, inflation, 0.0)
    left, right = factors(sums_ref[:half, :half] + shift)
    both = product(jnp.concatenate([left, right]), sums_ref[:half, half:])
    upper = both[half:]
    lower = sums_ref[half:, half:] - product(both[:half, :half], upper, 0, 0)
    upper = product(left, upper, 0, 0)
    left, right = factors(lower[:, :half] + shift)
    second = product(product(left, right, 0, 0), lower[:, half:])
    first = upper[:, half:] - product(upper[:, :half], second)
    mean = (
        jnp.sum(first, axis=0, keepdims=True) + jnp.sum(second, axis=0, keepdims=True)
    ) * (1.0 / members)
    weights_ref[:half] = (first - mean) * (1.0 / scale)
    weights_ref[half:] = (second - mean) * (1.0 / scale)
    chunk = log_ref.shape[0] // sems.shape[0]
    copies = []
    for n in range(sems.shape[0]):
        part = pl.ds(n * chunk, chunk)
        held_ref[part] = log_ref[part] + product(
            log_ref[part], weights_ref[...], precision=THREE_PASS
        )
        copies.append(pltpu.make_async_copy(held_ref.at[part], updated_hbm.at[part], sems.at[n]))
        copies[-1].start()
    for copy in copies:
        copy.wait()


def smooth(scale, *refs):
    *piece_refs, noise_ref, near_ref, log_ref, inner_ref, updated_hbm, final_hbm = refs[:-5]
    sums_ref, weights_ref, held_ref, sems, final_sem = refs[-5:]
    keep = pltpu.make_async_copy(inner_ref, final_hbm, final_sem)
    keep.start()
    sums_ref[...] = near_ref[...] + products(scale, piece_refs, noise_ref)
    update(scale, sums_ref, log_ref, updated_hbm, weights_ref, held_ref, sems)
    keep.wait()


def finish(scale, sums_ref, log_ref, inner_ref, updated_hbm, final_hbm, *scratch):
    weights_ref, held_ref, sems, final_sem = scratch
    keep = pltpu.make_async_copy(inner_ref, final_hbm, final_sem)
    keep.start()
    update(scale, sums_ref, log_ref, updated_hbm, weights_ref, held_ref, sems)
    keep.wait()


def assimilate(scale, pieces, noise, log_rows, final, sums):
    members = log_rows.shape[1]
    pair = (members, 2 * members)
    outs = (f32(*log_rows.shape), f32(*final.shape))
    scratch = [
        pltpu.VMEM((members, members), jnp.float32),
        pltpu.VMEM(log_rows.shape, jnp.float32),
        pltpu.SemaphoreType.DMA((4,)),
        pltpu.SemaphoreType.DMA,
    ]
    def partial(blocks, noise_rows):
        args = [*blocks, noise_rows]
        return call(
            functools.partial(partial_products, scale), "partial_products", f32(*pair),
            [VMEM] * len(args), args, flops=10**8,
        )

    if not sums:
        near = len(pieces) // 2
        split = sum(piece.shape[0] for piece in pieces[:near])
        args = [
            *pieces[near:], noise[split:], partial(pieces[:near], noise[:split]), log_rows, final
        ]
        return call(
            functools.partial(smooth, scale), "smooth", outs, [VMEM] * len(args), args,
            scratch=[pltpu.VMEM(pair, jnp.float32), *scratch], flops=10**9,
            out_specs=(HBM, HBM),
        )
    total = partial(pieces, noise)
    for route in sums:
        total = total + send(total, route)
    args = [total, log_rows, final]
    return call(
        functools.partial(finish, scale), "finish", outs, [VMEM] * 3, args,
        scratch=scratch, flops=10**9, out_specs=(HBM, HBM),
    )


def shards(
    initial_thermal_state,
    logarithmic_diffusivity,
    rock_class_code,
    rock_class_diffusivity,
    advection_courant,
    probe_locations,
    observed_readings,
    probe_noise_deviation,
    random_starters,
):
    span_x, span_y, depth, members = initial_thermal_state.shape
    rows = (span_x, span_y)
    cells = span_x * span_y
    temperature = initial_thermal_state.reshape(cells, depth, members)
    log_cond = logarithmic_diffusivity.reshape(cells, depth, members)
    tile = f32(cells, depth, members)
    faces = [(span_y, depth, members)] * 2 + [(span_x, depth, members)] * 2
    levels = rock_class_diffusivity.shape
    columns = -(-cells // 128) * 128
    temperature, log_cond, base, *sent = call(
        functools.partial(prepare, rows), "prepare",
        (tile, tile, f32(depth, columns), *(f32(2, *face) for face in faces)),
        [HBM] * 4,
        [
            pltpu.with_memory_space_constraint(array, pltpu.HBM)
            for array in (temperature, log_cond, rock_class_code, rock_class_diffusivity)
        ],
        scratch=[
            pltpu.VMEM((cells, depth, members), jnp.float32),
            pltpu.VMEM((columns, 128), jnp.float32),
            pltpu.VMEM(rock_class_code.shape, jnp.int32),
            pltpu.SMEM(levels, jnp.float32),
            pltpu.SemaphoreType.DMA((4,)),
        ],
    )
    got = exchange(sent)
    half_cond, middle = call(
        functools.partial(middle_inside, rows), "middle_inside", (tile, tile),
        [SMEM] + [VMEM] * 3, [advection_courant, temperature, log_cond, base],
        flops=10**7,
    )
    middle, *sent = call(
        functools.partial(middle_border, rows), "middle_border",
        (tile, *(f32(*face) for face in faces)),
        [SMEM] + [VMEM] * 7,
        [advection_courant, temperature, half_cond, *[got[n] for n in ORDER], middle],
        flops=10**7, aliases={7: 0},
    )
    got_middle = exchange(sent)
    final = call(
        functools.partial(final_inside, rows), "final_inside", tile,
        [SMEM] + [VMEM] * 2, [advection_courant, middle, half_cond], flops=10**7,
    )
    scale = (members - 1) ** 0.5
    obs_count = probe_locations.shape[0]
    final, scaled = call(
        functools.partial(observe, rows), "observe", (tile, f32(obs_count, members)),
        [SMEM] * 4 + [VMEM] * 11,
        [
            advection_courant, probe_locations, observed_readings,
            1.0 / (probe_noise_deviation * scale), middle, half_cond, *[got_middle[n] for n in ORDER], *[got[n] for n in ORDER], final,
        ],
        flops=10**7, aliases={14: 0},
    )
    count_x, count_y = lax.axis_size("gx"), lax.axis_size("gy")
    gathers, sums = plan_exchange(count_x, count_y, obs_count, 4 * members)
    pieces, owners = gather_blocks(scaled, gathers, count_x * count_y)
    owner = jnp.asarray(owners, jnp.int32)[lax.axis_index(("gx", "gy"))]
    obs_index = (
        owner[:, None] * obs_count + jnp.arange(obs_count, dtype=jnp.int32)[None, :]
    ).reshape(-1)
    noise = inflation**0.5 * perturbation(obs_index, random_starters)
    updated, final = assimilate(
        scale, pieces, noise, log_cond.reshape(-1, members), final, sums
    )
    shape = initial_thermal_state.shape
    return (final.reshape(shape), updated.reshape(shape))


def solution(mesh):
    placed = (
        P("gx", "gy", None, None),
        P("gx", "gy", None, None),
        P("gx", "gy", None),
        P(),
        P(),
        P(("gx", "gy")),
        P(("gx", "gy")),
        P(("gx", "gy")),
        P(),
    )
    return jax.shard_map(
        shards,
        mesh=mesh,
        in_specs=placed,
        out_specs=(P("gx", "gy", None, None), P("gx", "gy", None, None)),
        check_vma=False,
    )
```

```python
import functools

import jax
import jax.numpy as jnp
from jax import lax
from jax.experimental import pallas as pl
from jax.experimental.pallas import tpu as pltpu
from jax.sharding import PartitionSpec as P

inflation = 4.0
HIGHEST = lax.Precision.HIGHEST
THREE_PASS = lax.Precision.HIGH
VMEM = pl.BlockSpec(memory_space=pltpu.VMEM)
SMEM = pl.BlockSpec(memory_space=pltpu.SMEM)


ORDER = (0, 2, 3, 1)
AT = (0, 3, 1, 2)
HBM = pl.BlockSpec(memory_space=pltpu.HBM)


def f32(*shape):
    return jax.ShapeDtypeStruct(shape, jnp.float32)


def call(kernel, name, outs, specs, args, scratch=(), flops=0, out_specs=None, aliases={}):
    moved = sum(4 * a.size for a in args)
    return pl.pallas_call(
        kernel,
        out_shape=outs,
        in_specs=specs,
        out_specs=jax.tree.map(lambda _: VMEM, outs) if out_specs is None else out_specs,
        scratch_shapes=scratch,
        input_output_aliases=aliases,
        compiler_params=pltpu.CompilerParams(vmem_limit_bytes=20 << 20),
        cost_estimate=pl.CostEstimate(flops=flops, bytes_accessed=moved, transcendentals=0),
        name=name,
    )(*args)


def halo_routes(count_x, count_y):
    def flat(i, j):
        return i * count_y + j

    def turn(i, j):
        ahead = j + 1 if i % 2 == 0 else j - 1
        return (i, ahead) if 0 <= ahead < count_y else (i ^ 1, j)

    places = [(i, j) for i in range(count_x) for j in range(count_y)]
    right = [(flat(i, j), flat((i + 1) % count_x, j)) for i, j in places]
    along = [(flat(i, j), flat(*turn(i, j))) for i, j in places]
    return [right, back(right), along, back(along)]


def back(route):
    return [(b, a) for a, b in route]


def exchange(faces):
    routes = halo_routes(lax.axis_size("gx"), lax.axis_size("gy"))
    return [lax.ppermute(face, ("gx", "gy"), route) for face, route in zip(faces, routes)]


def border(rows, wanted):
    span_x, span_y = rows
    return [
        (x, y)
        for x in range(span_x)
        for y in range(span_y)
        if (x in (0, span_x - 1) or y in (0, span_y - 1)) == wanted
    ]


def is_even():
    return lax.rem(lax.axis_index("gx"), 2) == 0


def store_faces(field_ref, rows, put):
    span_x, span_y = rows
    even = is_even()
    for y in range(span_y):
        put(0, y, field_ref[(span_x - 1) * span_y + y])
        put(1, y, field_ref[y])
    for x in range(span_x):
        for route, at in (
            (2, jnp.where(even, span_y - 1, 0)),
            (3, jnp.where(even, 0, span_y - 1)),
        ):
            put(route, x, field_ref[x * span_y + at])


def conductivity(rows, cells, log_ref, columns_ref, h_ref):
    depth, members = log_ref.shape[1:]
    columns = columns_ref[...]
    for x, y in cells:
        cell = x * rows[1] + y
        base = jnp.broadcast_to(columns[:, cell : cell + 1], (depth, members))
        h_ref[cell] = base * jnp.exp(log_ref[cell])


def prepare(rows, t_hbm, log_hbm, code_hbm, rock_hbm, *rest):
    t_ref, log_ref, columns_ref, *face_refs, h_ref, turned, code_ref, rock_ref, sems = rest
    span_x, span_y = rows
    depth = t_ref.shape[1]
    half = log_ref.shape[0] // 2
    low, high = pl.ds(0, half), pl.ds(half, half)
    pairs = (
        (code_hbm, code_ref), (rock_hbm, rock_ref), (log_hbm.at[low], log_ref.at[low]),
        (log_hbm.at[high], log_ref.at[high]), (t_hbm, t_ref),
    )
    copies = [
        pltpu.make_async_copy(source, target, sems.at[n])
        for n, (source, target) in enumerate(
            pairs
        )
    ]
    for copy in copies:
        copy.start()
    turned[...] = jnp.zeros_like(turned)
    copies[0].wait()
    copies[1].wait()
    for x in range(span_x):
        code = code_ref[x]
        base = jnp.zeros(code.shape, jnp.float32)
        for level in range(rock_ref.shape[0]):
            base = jnp.where(code == level, 0.5 * rock_ref[level], base)
        turned[x * span_y : (x + 1) * span_y, :depth] = base
    columns_ref[...] = jnp.transpose(turned[...])[:depth]
    cells = border(rows, True)
    copies[2].wait()
    conductivity(rows, [c for c in cells if c[0] * span_y < half], log_ref, columns_ref, h_ref)
    copies[3].wait()
    conductivity(rows, [c for c in cells if c[0] * span_y >= half], log_ref, columns_ref, h_ref)

    def put(field):
        def store(n, k, layer):
            face_refs[n][field, k] = layer

        return store

    store_faces(h_ref, rows, put(1))
    copies[4].wait()
    store_faces(t_ref, rows, put(0))


def advance(rows, cells, courant_ref, u_ref, h_ref, u_faces, h_faces, write):
    span_x, span_y = rows
    shape = u_ref.shape[1:]
    depth = shape[0]
    level = lax.broadcasted_iota(jnp.int32, shape, 0)
    courant = jnp.zeros(shape, jnp.float32)
    for z in range(depth):
        courant = jnp.where(level == z, courant_ref[z], courant)
    even = is_even()

    def beyond(faces, axis, after, k):
        name = ("gx", "gy")[axis]
        edge = lax.axis_index(name) == (lax.axis_size(name) - 1 if after else 0)
        if axis == 0:
            layer = faces(1 if after else 0, k)
        else:
            layer = jnp.where(even == after, faces(3, k), faces(2, k))
        return jnp.where(edge, 0.0, layer)

    def at(ref, faces, x, y):
        if x < 0 or x == span_x:
            return beyond(faces, 0, x > 0, y)
        if y < 0 or y == span_y:
            return beyond(faces, 1, y > 0, x)
        return ref[x * span_y + y]

    before, from_before = None, None
    for x, y in cells:
        u, h = u_ref[x * span_y + y], h_ref[x * span_y + y]

        def flow(i, j):
            step = at(u_ref, u_faces, i, j) - u
            return step, (h + at(h_ref, h_faces, i, j)) * step

        rise = jnp.where(level == depth - 1, 0.0, pltpu.roll(u, depth - 1, 0)) - u
        lift = (h + jnp.where(level == depth - 1, 0.0, pltpu.roll(h, depth - 1, 0))) * rise
        sink = jnp.where(level == 0, h * u, pltpu.roll(lift, 1, 0))
        west, from_west = flow(x - 1, y)
        from_east = flow(x + 1, y)[1]
        from_north = flow(x, y + 1)[1]
        from_south = from_before if before == (x, y - 1) else flow(x, y - 1)[1]
        before, from_before = (x, y), -from_north
        change = (from_east + from_west) + (from_north + from_south) + (lift - sink)
        write(x * span_y + y, u + change + courant * west)


def into(ref):
    def write(cell, value):
        ref[cell] = value

    return write


def middle_inside(rows, courant_ref, t_ref, log_ref, columns_ref, h_ref, middle_ref):
    inside = border(rows, False)
    conductivity(rows, border(rows, True) + inside, log_ref, columns_ref, h_ref)
    advance(rows, inside, courant_ref, t_ref, h_ref, None, None, into(middle_ref))


def middle_border(rows, courant_ref, t_ref, h_ref, *rest):
    got, middle_ref, face_refs = rest[:4], rest[5], rest[6:]
    advance(
        rows, border(rows, True), courant_ref, t_ref, h_ref,
        lambda n, k: got[AT[n]][0, k], lambda n, k: got[AT[n]][1, k], into(middle_ref),
    )

    def put(n, k, layer):
        face_refs[n][k] = layer

    store_faces(middle_ref, rows, put)


def final_inside(rows, courant_ref, u_ref, h_ref, final_ref):
    advance(rows, border(rows, False), courant_ref, u_ref, h_ref, None, None, into(final_ref))


def observe(rows, courant_ref, cells_ref, reading_ref, factor_ref, u_ref, h_ref, *rest):
    got_u, got_h, final_ref, scaled_ref = rest[:4], rest[4:8], rest[9], rest[10]
    depth = u_ref.shape[1]
    advance(
        rows, border(rows, True), courant_ref, u_ref, h_ref,
        lambda n, k: got_u[AT[n]][k], lambda n, k: got_h[AT[n]][1, k], into(final_ref),
    )
    for j in range(scaled_ref.shape[0]):
        cell = cells_ref[j]
        row = final_ref[lax.div(cell, depth), pl.ds(lax.rem(cell, depth), 1), :]
        scaled_ref[j : j + 1, :] = (row - reading_ref[j]) * factor_ref[j]


def modulo(value, divisor):
    quotient = (value.astype(jnp.float32) * (1.0 / divisor)).astype(jnp.int32)
    rest = value - quotient * divisor
    rest = jnp.where(rest < 0, rest + divisor, rest)
    return jnp.where(rest >= divisor, rest - divisor, rest)


def perturbation(obs_index, random_starters):
    first = random_starters * 7919 % 65521
    second = obs_index * 331 % 65521
    hashed = modulo(
        first[None, :] * (second[:, None] % 32749) + first[None, :] + second[:, None], 65521
    )
    uniform_value = (hashed.astype(jnp.float32) + 0.5) / 65521.0
    return jnp.sqrt(3.0) * (2.0 * uniform_value - 1.0)


def plan_exchange(count_x, count_y, rows, limit):
    def route(move):
        return [
            (i * count_y + j, a * count_y + b)
            for i in range(count_x)
            for j in range(count_y)
            for a, b in [move(i, j)]
        ]

    def shifted(axis, i, j, step):
        return (i ^ step, j) if axis == "gx" else (i, j ^ step)

    def across(axis, step):
        def move(i, j):
            at = i if axis == "gx" else j
            a, b = shifted(axis, i, j, step)
            return (a, b) if at < at ^ step else (a ^ 1, b)

        return route(move)

    def around(axis, low, high):
        def move(i, j):
            at = i if axis == "gx" else j
            step = low if bool(at & low) == bool(at & high) else high
            return shifted(axis, i, j, step)

        return route(move)

    gathers, sums = [], []
    for axis, count in (("gy", count_y), ("gx", count_x)):
        bits = [1 << b for b in range(count.bit_length() - 1)]
        while bits:
            if len(bits) > 1 and rows * 4 <= limit:
                high, low = bits.pop(), bits.pop()
                ring = around(axis, low, high)
                gathers.append([ring, back(ring), across(axis, low | high)])
                rows *= 4
                continue
            step = bits.pop()
            swap = route(functools.partial(shifted, axis, step=step))
            if rows * 2 <= limit:
                gathers.append([swap])
                rows *= 2
            else:
                sums.append(swap)
    return gathers, sums


def send(block, route):
    return lax.ppermute(block, ("gx", "gy"), route)


def pack(*refs):
    start = 0
    for ref in refs[:-1]:
        refs[-1][start : start + ref.shape[0], :] = ref[...]
        start += ref.shape[0]


def gather_blocks(block, gathers, devices):
    pieces, owners = [block], [[d] for d in range(devices)]
    for routes in gathers:
        if len(routes) > 1 and len(pieces) > 1:
            rows = sum(piece.shape[0] for piece in pieces)
            pieces = [
                call(pack, "pack", f32(rows, block.shape[1]), [VMEM] * len(pieces), pieces)
            ]
        pieces = pieces + [send(piece, route) for route in routes for piece in pieces]
        held = [list(own) for own in owners]
        for route in routes:
            for source, target in route:
                held[target] += owners[source]
        owners = held
    return pieces, owners


def product(a, b, over_a=1, over_b=0, precision=HIGHEST):
    return lax.dot_general(
        a, b, (((over_a,), (over_b,)), ((), ())), precision=precision,
        preferred_element_type=jnp.float32,
    )


def tree_sum(terms):
    while len(terms) > 1:
        terms = [sum(terms[n : n + 2]) for n in range(0, len(terms), 2)]
    return terms[0]


def factors(block):
    size, group = block.shape[0], 16
    shape = (group, size)
    lane = lax.broadcasted_iota(jnp.int32, shape, 1)
    sub = lax.broadcasted_iota(jnp.int32, shape, 0)
    count = size // group
    rows = [block[group * i : group * (i + 1), :] for i in range(count)]
    left, right = [], []

    def spread(values, at):
        return jnp.broadcast_to(values[:, at : at + 1], shape)

    for g in range(count):
        first = group * g
        inside = (lane >= first) & (lane < first + group)
        unit = jnp.where(lane - first == sub, 1.0, 0.0)
        columns = [spread(rows[g], first + q) for q in range(group)]
        held = jnp.where(inside, unit, rows[g])
        left.append(jnp.where(lane < first, rows[g], unit))
        for p in range(group):
            pivot = 1.0 / columns[p][p : p + 1, :]
            for q in range(p + 1, group):
                scaled = columns[q][p : p + 1, :] * pivot
                columns[q] = jnp.where(sub == p, scaled, columns[q] - columns[p] * scaled)
            scaled = held[p : p + 1, :] * pivot
            held = jnp.where(sub == p, scaled, held - columns[p] * scaled)
        right.append(jnp.where(lane < first + group, held, 0.0))
        for i in range(g + 1, count):
            rows[i] = jnp.where(inside, 0.0, rows[i]) - tree_sum(
                [spread(rows[i], first + q) * held[q : q + 1, :] for q in range(group)]
            )
    return jnp.concatenate(left), jnp.concatenate(right)


def products(scale, piece_refs, noise_ref):
    scaled = jnp.concatenate([ref[...] for ref in piece_refs])
    members = scaled.shape[1]
    spread = scaled - jnp.sum(scaled, axis=1, keepdims=True) * (1.0 / members)
    misfit = noise_ref[...] - scale * scaled
    return product(spread, jnp.concatenate([spread, misfit], axis=1), 0, 0, THREE_PASS)


def partial_products(scale, *refs):
    *piece_refs, noise_ref, sums_ref = refs
    sums_ref[...] = products(scale, piece_refs, noise_ref)


def update(scale, sums_ref, log_ref, updated_hbm, weights_ref, held_ref, sems):
    members = weights_ref.shape[0]
    half = members // 2
    diagonal = lax.broadcasted_iota(jnp.int32, (half, half), 0) == lax.broadcasted_iota(
        jnp.int32, (half, half), 1
    )
    shift = jnp.where(diagonal, inflation, 0.0)
    left, right = factors(sums_ref[:half, :half] + shift)
    both = product(jnp.concatenate([left, right]), sums_ref[:half, half:])
    upper = both[half:]
    lower = sums_ref[half:, half:] - product(both[:half, :half], upper, 0, 0)
    upper = product(left, upper, 0, 0)
    left, right = factors(lower[:, :half] + shift)
    second = product(product(left, right, 0, 0), lower[:, half:])
    first = upper[:, half:] - product(upper[:, :half], second)
    mean = (
        jnp.sum(first, axis=0, keepdims=True) + jnp.sum(second, axis=0, keepdims=True)
    ) * (1.0 / members)
    weights_ref[:half] = (first - mean) * (1.0 / scale)
    weights_ref[half:] = (second - mean) * (1.0 / scale)
    chunk = log_ref.shape[0] // sems.shape[0]
    copies = []
    for n in range(sems.shape[0]):
        part = pl.ds(n * chunk, chunk)
        held_ref[part] = log_ref[part] + product(
            log_ref[part], weights_ref[...], precision=THREE_PASS
        )
        copies.append(pltpu.make_async_copy(held_ref.at[part], updated_hbm.at[part], sems.at[n]))
        copies[-1].start()
    for copy in copies:
        copy.wait()


def smooth(scale, *refs):
    *piece_refs, noise_ref, near_ref, log_ref, inner_ref, updated_hbm, final_hbm = refs[:-5]
    sums_ref, weights_ref, held_ref, sems, final_sem = refs[-5:]
    keep = pltpu.make_async_copy(inner_ref, final_hbm, final_sem)
    keep.start()
    sums_ref[...] = near_ref[...] + products(scale, piece_refs, noise_ref)
    update(scale, sums_ref, log_ref, updated_hbm, weights_ref, held_ref, sems)
    keep.wait()


def finish(scale, sums_ref, log_ref, inner_ref, updated_hbm, final_hbm, *scratch):
    weights_ref, held_ref, sems, final_sem = scratch
    keep = pltpu.make_async_copy(inner_ref, final_hbm, final_sem)
    keep.start()
    update(scale, sums_ref, log_ref, updated_hbm, weights_ref, held_ref, sems)
    keep.wait()


def assimilate(scale, pieces, noise, log_rows, final, sums):
    members = log_rows.shape[1]
    pair = (members, 2 * members)
    outs = (f32(*log_rows.shape), f32(*final.shape))
    scratch = [
        pltpu.VMEM((members, members), jnp.float32),
        pltpu.VMEM(log_rows.shape, jnp.float32),
        pltpu.SemaphoreType.DMA((4,)),
        pltpu.SemaphoreType.DMA,
    ]
    def partial(blocks, noise_rows):
        args = [*blocks, noise_rows]
        return call(
            functools.partial(partial_products, scale), "partial_products", f32(*pair),
            [VMEM] * len(args), args, flops=10**8,
        )

    if not sums:
        near = len(pieces) // 2
        split = sum(piece.shape[0] for piece in pieces[:near])
        args = [
            *pieces[near:], noise[split:], partial(pieces[:near], noise[:split]), log_rows, final
        ]
        return call(
            functools.partial(smooth, scale), "smooth", outs, [VMEM] * len(args), args,
            scratch=[pltpu.VMEM(pair, jnp.float32), *scratch], flops=10**9,
            out_specs=(HBM, HBM),
        )
    total = partial(pieces, noise)
    for route in sums:
        total = total + send(total, route)
    args = [total, log_rows, final]
    return call(
        functools.partial(finish, scale), "finish", outs, [VMEM] * 3, args,
        scratch=scratch, flops=10**9, out_specs=(HBM, HBM),
    )


def shards(
    initial_thermal_state,
    logarithmic_diffusivity,
    rock_class_code,
    rock_class_diffusivity,
    advection_courant,
    probe_locations,
    observed_readings,
    probe_noise_deviation,
    random_starters,
):
    span_x, span_y, depth, members = initial_thermal_state.shape
    rows = (span_x, span_y)
    cells = span_x * span_y
    temperature = initial_thermal_state.reshape(cells, depth, members)
    log_cond = logarithmic_diffusivity.reshape(cells, depth, members)
    tile = f32(cells, depth, members)
    faces = [(span_y, depth, members)] * 2 + [(span_x, depth, members)] * 2
    levels = rock_class_diffusivity.shape
    columns = -(-cells // 128) * 128
    temperature, log_cond, base, *sent = call(
        functools.partial(prepare, rows), "prepare",
        (tile, tile, f32(depth, columns), *(f32(2, *face) for face in faces)),
        [HBM] * 4,
        [
            pltpu.with_memory_space_constraint(array, pltpu.HBM)
            for array in (temperature, log_cond, rock_class_code, rock_class_diffusivity)
        ],
        scratch=[
            pltpu.VMEM((cells, depth, members), jnp.float32),
            pltpu.VMEM((columns, 128), jnp.float32),
            pltpu.VMEM(rock_class_code.shape, jnp.int32),
            pltpu.SMEM(levels, jnp.float32),
            pltpu.SemaphoreType.DMA((5,)),
        ],
    )
    got = exchange(sent)
    half_cond, middle = call(
        functools.partial(middle_inside, rows), "middle_inside", (tile, tile),
        [SMEM] + [VMEM] * 3, [advection_courant, temperature, log_cond, base],
        flops=10**7,
    )
    middle, *sent = call(
        functools.partial(middle_border, rows), "middle_border",
        (tile, *(f32(*face) for face in faces)),
        [SMEM] + [VMEM] * 7,
        [advection_courant, temperature, half_cond, *[got[n] for n in ORDER], middle],
        flops=10**7, aliases={7: 0},
    )
    got_middle = exchange(sent)
    final = call(
        functools.partial(final_inside, rows), "final_inside", tile,
        [SMEM] + [VMEM] * 2, [advection_courant, middle, half_cond], flops=10**7,
    )
    scale = (members - 1) ** 0.5
    obs_count = probe_locations.shape[0]
    final, scaled = call(
        functools.partial(observe, rows), "observe", (tile, f32(obs_count, members)),
        [SMEM] * 4 + [VMEM] * 11,
        [
            advection_courant, probe_locations, observed_readings,
            1.0 / (probe_noise_deviation * scale), middle, half_cond, *[got_middle[n] for n in ORDER], *[got[n] for n in ORDER], final,
        ],
        flops=10**7, aliases={14: 0},
    )
    count_x, count_y = lax.axis_size("gx"), lax.axis_size("gy")
    gathers, sums = plan_exchange(count_x, count_y, obs_count, 4 * members)
    pieces, owners = gather_blocks(scaled, gathers, count_x * count_y)
    owner = jnp.asarray(owners, jnp.int32)[lax.axis_index(("gx", "gy"))]
    obs_index = (
        owner[:, None] * obs_count + jnp.arange(obs_count, dtype=jnp.int32)[None, :]
    ).reshape(-1)
    noise = inflation**0.5 * perturbation(obs_index, random_starters)
    updated, final = assimilate(
        scale, pieces, noise, log_cond.reshape(-1, members), final, sums
    )
    shape = initial_thermal_state.shape
    return (final.reshape(shape), updated.reshape(shape))


def solution(mesh):
    placed = (
        P("gx", "gy", None, None),
        P("gx", "gy", None, None),
        P("gx", "gy", None),
        P(),
        P(),
        P(("gx", "gy")),
        P(("gx", "gy")),
        P(("gx", "gy")),
        P(),
    )
    return jax.shard_map(
        shards,
        mesh=mesh,
        in_specs=placed,
        out_specs=(P("gx", "gy", None, None), P("gx", "gy", None, None)),
        check_vma=False,
    )
```

```python
import functools

import jax
import jax.numpy as jnp
from jax import lax
from jax.experimental import pallas as pl
from jax.experimental.pallas import tpu as pltpu
from jax.sharding import PartitionSpec as P

inflation = 4.0
HIGHEST = lax.Precision.HIGHEST
THREE_PASS = lax.Precision.HIGH
VMEM = pl.BlockSpec(memory_space=pltpu.VMEM)
SMEM = pl.BlockSpec(memory_space=pltpu.SMEM)


ORDER = (0, 2, 3, 1)
AT = (0, 3, 1, 2)
HBM = pl.BlockSpec(memory_space=pltpu.HBM)


def f32(*shape):
    return jax.ShapeDtypeStruct(shape, jnp.float32)


def call(kernel, name, outs, specs, args, scratch=(), flops=0, out_specs=None, aliases={}):
    moved = sum(4 * a.size for a in args)
    return pl.pallas_call(
        kernel,
        out_shape=outs,
        in_specs=specs,
        out_specs=jax.tree.map(lambda _: VMEM, outs) if out_specs is None else out_specs,
        scratch_shapes=scratch,
        input_output_aliases=aliases,
        compiler_params=pltpu.CompilerParams(vmem_limit_bytes=20 << 20),
        cost_estimate=pl.CostEstimate(flops=flops, bytes_accessed=moved, transcendentals=0),
        name=name,
    )(*args)


def halo_routes(count_x, count_y):
    def flat(i, j):
        return i * count_y + j

    def turn(i, j):
        ahead = j + 1 if i % 2 == 0 else j - 1
        return (i, ahead) if 0 <= ahead < count_y else (i ^ 1, j)

    places = [(i, j) for i in range(count_x) for j in range(count_y)]
    right = [(flat(i, j), flat((i + 1) % count_x, j)) for i, j in places]
    along = [(flat(i, j), flat(*turn(i, j))) for i, j in places]
    return [right, back(right), along, back(along)]


def back(route):
    return [(b, a) for a, b in route]


def exchange(faces):
    routes = halo_routes(lax.axis_size("gx"), lax.axis_size("gy"))
    return [lax.ppermute(face, ("gx", "gy"), route) for face, route in zip(faces, routes)]


def border(rows, wanted):
    span_x, span_y = rows
    return [
        (x, y)
        for x in range(span_x)
        for y in range(span_y)
        if (x in (0, span_x - 1) or y in (0, span_y - 1)) == wanted
    ]


def is_even():
    return lax.rem(lax.axis_index("gx"), 2) == 0


def store_faces(field_ref, rows, put):
    span_x, span_y = rows
    even = is_even()
    for y in range(span_y):
        put(0, y, field_ref[(span_x - 1) * span_y + y])
        put(1, y, field_ref[y])
    for x in range(span_x):
        for route, at in (
            (2, jnp.where(even, span_y - 1, 0)),
            (3, jnp.where(even, 0, span_y - 1)),
        ):
            put(route, x, field_ref[x * span_y + at])


def conductivity(rows, cells, log_ref, columns_ref, h_ref):
    depth, members = log_ref.shape[1:]
    columns = columns_ref[...]
    for x, y in cells:
        cell = x * rows[1] + y
        base = jnp.broadcast_to(columns[:, cell : cell + 1], (depth, members))
        h_ref[cell] = base * jnp.exp(log_ref[cell])


def prepare(rows, t_hbm, log_hbm, code_hbm, rock_hbm, *rest):
    t_ref, log_ref, columns_ref, *face_refs, h_ref, turned, code_ref, rock_ref, sems = rest
    span_x, span_y = rows
    depth = t_ref.shape[1]
    half = log_ref.shape[0] // 2
    low, high = pl.ds(0, half), pl.ds(half, half)
    pairs = (
        (code_hbm, code_ref), (rock_hbm, rock_ref), (log_hbm.at[low], log_ref.at[low]),
        (log_hbm.at[high], log_ref.at[high]), (t_hbm, t_ref),
    )
    copies = [
        pltpu.make_async_copy(source, target, sems.at[n])
        for n, (source, target) in enumerate(
            pairs
        )
    ]
    for copy in copies:
        copy.start()
    turned[...] = jnp.zeros_like(turned)
    copies[0].wait()
    copies[1].wait()
    for x in range(span_x):
        code = code_ref[x]
        base = jnp.zeros(code.shape, jnp.float32)
        for level in range(rock_ref.shape[0]):
            base = jnp.where(code == level, 0.5 * rock_ref[level], base)
        turned[x * span_y : (x + 1) * span_y, :depth] = base
    columns_ref[...] = jnp.transpose(turned[...])[:depth]
    cells = border(rows, True)
    copies[2].wait()
    conductivity(rows, [c for c in cells if c[0] * span_y < half], log_ref, columns_ref, h_ref)
    copies[3].wait()
    conductivity(rows, [c for c in cells if c[0] * span_y >= half], log_ref, columns_ref, h_ref)

    def put(field):
        def store(n, k, layer):
            face_refs[n][field, k] = layer

        return store

    store_faces(h_ref, rows, put(1))
    copies[4].wait()
    store_faces(t_ref, rows, put(0))


def advance(rows, cells, courant_ref, u_ref, h_ref, u_faces, h_faces, write):
    span_x, span_y = rows
    shape = u_ref.shape[1:]
    depth = shape[0]
    level = lax.broadcasted_iota(jnp.int32, shape, 0)
    courant = jnp.zeros(shape, jnp.float32)
    for z in range(depth):
        courant = jnp.where(level == z, courant_ref[z], courant)
    even = is_even()

    def beyond(faces, axis, after, k):
        name = ("gx", "gy")[axis]
        edge = lax.axis_index(name) == (lax.axis_size(name) - 1 if after else 0)
        if axis == 0:
            layer = faces(1 if after else 0, k)
        else:
            layer = jnp.where(even == after, faces(3, k), faces(2, k))
        return jnp.where(edge, 0.0, layer)

    def at(ref, faces, x, y):
        if x < 0 or x == span_x:
            return beyond(faces, 0, x > 0, y)
        if y < 0 or y == span_y:
            return beyond(faces, 1, y > 0, x)
        return ref[x * span_y + y]

    before, from_before = None, None
    for x, y in cells:
        u, h = u_ref[x * span_y + y], h_ref[x * span_y + y]

        def flow(i, j):
            step = at(u_ref, u_faces, i, j) - u
            return step, (h + at(h_ref, h_faces, i, j)) * step

        rise = jnp.where(level == depth - 1, 0.0, pltpu.roll(u, depth - 1, 0)) - u
        lift = (h + jnp.where(level == depth - 1, 0.0, pltpu.roll(h, depth - 1, 0))) * rise
        sink = jnp.where(level == 0, h * u, pltpu.roll(lift, 1, 0))
        west, from_west = flow(x - 1, y)
        from_east = flow(x + 1, y)[1]
        from_north = flow(x, y + 1)[1]
        from_south = from_before if before == (x, y - 1) else flow(x, y - 1)[1]
        before, from_before = (x, y), -from_north
        change = (from_east + from_west) + (from_north + from_south) + (lift - sink)
        write(x * span_y + y, u + change + courant * west)


def into(ref):
    def write(cell, value):
        ref[cell] = value

    return write


def middle_inside(rows, courant_ref, t_ref, log_ref, columns_ref, h_ref, middle_ref):
    inside = border(rows, False)
    conductivity(rows, border(rows, True) + inside, log_ref, columns_ref, h_ref)
    advance(rows, inside, courant_ref, t_ref, h_ref, None, None, into(middle_ref))


def middle_border(rows, courant_ref, t_ref, h_ref, *rest):
    got, middle_ref, face_refs = rest[:4], rest[5], rest[6:]
    advance(
        rows, border(rows, True), courant_ref, t_ref, h_ref,
        lambda n, k: got[AT[n]][0, k], lambda n, k: got[AT[n]][1, k], into(middle_ref),
    )

    def put(n, k, layer):
        face_refs[n][k] = layer

    store_faces(middle_ref, rows, put)


def final_inside(rows, courant_ref, u_ref, h_ref, final_ref):
    advance(rows, border(rows, False), courant_ref, u_ref, h_ref, None, None, into(final_ref))


def observe(rows, courant_ref, cells_ref, reading_ref, factor_ref, u_ref, h_ref, *rest):
    got_u, got_h, final_ref, scaled_ref = rest[:4], rest[4:8], rest[9], rest[10]
    depth = u_ref.shape[1]
    advance(
        rows, border(rows, True), courant_ref, u_ref, h_ref,
        lambda n, k: got_u[AT[n]][k], lambda n, k: got_h[AT[n]][1, k], into(final_ref),
    )
    for j in range(scaled_ref.shape[0]):
        cell = cells_ref[j]
        row = final_ref[lax.div(cell, depth), pl.ds(lax.rem(cell, depth), 1), :]
        scaled_ref[j : j + 1, :] = (row - reading_ref[j]) * factor_ref[j]


def modulo(value, divisor):
    quotient = (value.astype(jnp.float32) * (1.0 / divisor)).astype(jnp.int32)
    rest = value - quotient * divisor
    rest = jnp.where(rest < 0, rest + divisor, rest)
    return jnp.where(rest >= divisor, rest - divisor, rest)


def perturbation(obs_index, random_starters):
    first = random_starters * 7919 % 65521
    second = obs_index * 331 % 65521
    hashed = modulo(
        first[None, :] * (second[:, None] % 32749) + first[None, :] + second[:, None], 65521
    )
    uniform_value = (hashed.astype(jnp.float32) + 0.5) / 65521.0
    return jnp.sqrt(3.0) * (2.0 * uniform_value - 1.0)


def plan_exchange(count_x, count_y, rows, limit):
    def route(move):
        return [
            (i * count_y + j, a * count_y + b)
            for i in range(count_x)
            for j in range(count_y)
            for a, b in [move(i, j)]
        ]

    def shifted(axis, i, j, step):
        return (i ^ step, j) if axis == "gx" else (i, j ^ step)

    def across(axis, step):
        def move(i, j):
            at = i if axis == "gx" else j
            a, b = shifted(axis, i, j, step)
            return (a, b) if at < at ^ step else (a ^ 1, b)

        return route(move)

    def around(axis, low, high):
        def move(i, j):
            at = i if axis == "gx" else j
            step = low if bool(at & low) == bool(at & high) else high
            return shifted(axis, i, j, step)

        return route(move)

    gathers, sums = [], []
    for axis, count in (("gy", count_y), ("gx", count_x)):
        bits = [1 << b for b in range(count.bit_length() - 1)]
        while bits:
            if len(bits) > 1 and rows * 4 <= limit:
                high, low = bits.pop(), bits.pop()
                ring = around(axis, low, high)
                gathers.append([ring, back(ring), across(axis, low | high)])
                rows *= 4
                continue
            step = bits.pop()
            swap = route(functools.partial(shifted, axis, step=step))
            if rows * 2 <= limit:
                gathers.append([swap])
                rows *= 2
            else:
                sums.append(swap)
    return gathers, sums


def send(block, route):
    return lax.ppermute(block, ("gx", "gy"), route)


def pack(*refs):
    start = 0
    for ref in refs[:-1]:
        refs[-1][start : start + ref.shape[0], :] = ref[...]
        start += ref.shape[0]


def gather_blocks(block, gathers, devices):
    pieces, owners = [block], [[d] for d in range(devices)]
    for routes in gathers:
        if len(routes) > 1 and len(pieces) > 1:
            rows = sum(piece.shape[0] for piece in pieces)
            pieces = [
                call(pack, "pack", f32(rows, block.shape[1]), [VMEM] * len(pieces), pieces)
            ]
        pieces = pieces + [send(piece, route) for route in routes for piece in pieces]
        held = [list(own) for own in owners]
        for route in routes:
            for source, target in route:
                held[target] += owners[source]
        owners = held
    return pieces, owners


def product(a, b, over_a=1, over_b=0, precision=HIGHEST):
    return lax.dot_general(
        a, b, (((over_a,), (over_b,)), ((), ())), precision=precision,
        preferred_element_type=jnp.float32,
    )


def tree_sum(terms):
    while len(terms) > 1:
        terms = [sum(terms[n : n + 2]) for n in range(0, len(terms), 2)]
    return terms[0]


def factors(block):
    size, group = block.shape[0], 16
    shape = (group, size)
    lane = lax.broadcasted_iota(jnp.int32, shape, 1)
    sub = lax.broadcasted_iota(jnp.int32, shape, 0)
    count = size // group
    rows = [block[group * i : group * (i + 1), :] for i in range(count)]
    left, right = [], []

    def spread(values, at):
        return jnp.broadcast_to(values[:, at : at + 1], shape)

    for g in range(count):
        first = group * g
        inside = (lane >= first) & (lane < first + group)
        unit = jnp.where(lane - first == sub, 1.0, 0.0)
        columns = [spread(rows[g], first + q) for q in range(group)]
        held = jnp.where(inside, unit, rows[g])
        left.append(jnp.where(lane < first, rows[g], unit))
        for p in range(group):
            pivot = 1.0 / columns[p][p : p + 1, :]
            for q in range(p + 1, group):
                scaled = columns[q][p : p + 1, :] * pivot
                columns[q] = jnp.where(sub == p, scaled, columns[q] - columns[p] * scaled)
            scaled = held[p : p + 1, :] * pivot
            held = jnp.where(sub == p, scaled, held - columns[p] * scaled)
        right.append(jnp.where(lane < first + group, held, 0.0))
        for i in range(g + 1, count):
            rows[i] = jnp.where(inside, 0.0, rows[i]) - tree_sum(
                [spread(rows[i], first + q) * held[q : q + 1, :] for q in range(group)]
            )
    return jnp.concatenate(left), jnp.concatenate(right)


def products(scale, piece_refs, noise_ref):
    scaled = jnp.concatenate([ref[...] for ref in piece_refs])
    members = scaled.shape[1]
    spread = scaled - jnp.sum(scaled, axis=1, keepdims=True) * (1.0 / members)
    misfit = noise_ref[...] - scale * scaled
    half = members // 2
    right = jnp.concatenate([spread, misfit], axis=1)
    upper = product(spread[:, :half], right, 0, 0, THREE_PASS)
    lower = product(spread[:, half:], right[:, half:], 0, 0, THREE_PASS)
    return upper, lower


def partial_products(scale, *refs):
    *piece_refs, noise_ref, sums_ref = refs
    half = sums_ref.shape[0] // 2
    sums_ref[half:, :half] = jnp.zeros((half, half), jnp.float32)
    sums_ref[:half], sums_ref[half:, half:] = products(scale, piece_refs, noise_ref)


def update(scale, sums_ref, log_ref, updated_hbm, weights_ref, held_ref, sems):
    members = weights_ref.shape[0]
    half = members // 2
    diagonal = lax.broadcasted_iota(jnp.int32, (half, half), 0) == lax.broadcasted_iota(
        jnp.int32, (half, half), 1
    )
    shift = jnp.where(diagonal, inflation, 0.0)
    left, right = factors(sums_ref[:half, :half] + shift)
    both = product(jnp.concatenate([left, right]), sums_ref[:half, half:])
    upper = both[half:]
    lower = sums_ref[half:, half:] - product(both[:half, :half], upper, 0, 0)
    upper = product(left, upper, 0, 0)
    left, right = factors(lower[:, :half] + shift)
    second = product(product(left, right, 0, 0), lower[:, half:])
    first = upper[:, half:] - product(upper[:, :half], second)
    mean = (
        jnp.sum(first, axis=0, keepdims=True) + jnp.sum(second, axis=0, keepdims=True)
    ) * (1.0 / members)
    weights_ref[:half] = (first - mean) * (1.0 / scale)
    weights_ref[half:] = (second - mean) * (1.0 / scale)
    chunk = log_ref.shape[0] // sems.shape[0]
    copies = []
    for n in range(sems.shape[0]):
        part = pl.ds(n * chunk, chunk)
        held_ref[part] = log_ref[part] + product(
            log_ref[part], weights_ref[...], precision=THREE_PASS
        )
        copies.append(pltpu.make_async_copy(held_ref.at[part], updated_hbm.at[part], sems.at[n]))
        copies[-1].start()
    for copy in copies:
        copy.wait()


def smooth(scale, *refs):
    *piece_refs, noise_ref, near_ref, log_ref, inner_ref, updated_hbm, final_hbm = refs[:-5]
    sums_ref, weights_ref, held_ref, sems, final_sem = refs[-5:]
    keep = pltpu.make_async_copy(inner_ref, final_hbm, final_sem)
    keep.start()
    half = sums_ref.shape[0] // 2
    upper, lower = products(scale, piece_refs, noise_ref)
    sums_ref[:half] = near_ref[:half] + upper
    sums_ref[half:, half:] = near_ref[half:, half:] + lower
    update(scale, sums_ref, log_ref, updated_hbm, weights_ref, held_ref, sems)
    keep.wait()


def finish(scale, sums_ref, log_ref, inner_ref, updated_hbm, final_hbm, *scratch):
    weights_ref, held_ref, sems, final_sem = scratch
    keep = pltpu.make_async_copy(inner_ref, final_hbm, final_sem)
    keep.start()
    update(scale, sums_ref, log_ref, updated_hbm, weights_ref, held_ref, sems)
    keep.wait()


def assimilate(scale, pieces, noise, log_rows, final, sums):
    members = log_rows.shape[1]
    pair = (members, 2 * members)
    outs = (f32(*log_rows.shape), f32(*final.shape))
    scratch = [
        pltpu.VMEM((members, members), jnp.float32),
        pltpu.VMEM(log_rows.shape, jnp.float32),
        pltpu.SemaphoreType.DMA((4,)),
        pltpu.SemaphoreType.DMA,
    ]
    def partial(blocks, noise_rows):
        args = [*blocks, noise_rows]
        return call(
            functools.partial(partial_products, scale), "partial_products", f32(*pair),
            [VMEM] * len(args), args, flops=10**8,
        )

    if not sums:
        near = len(pieces) // 2
        split = sum(piece.shape[0] for piece in pieces[:near])
        args = [
            *pieces[near:], noise[split:], partial(pieces[:near], noise[:split]), log_rows, final
        ]
        return call(
            functools.partial(smooth, scale), "smooth", outs, [VMEM] * len(args), args,
            scratch=[pltpu.VMEM(pair, jnp.float32), *scratch], flops=10**9,
            out_specs=(HBM, HBM),
        )
    total = partial(pieces, noise)
    for route in sums:
        total = total + send(total, route)
    args = [total, log_rows, final]
    return call(
        functools.partial(finish, scale), "finish", outs, [VMEM] * 3, args,
        scratch=scratch, flops=10**9, out_specs=(HBM, HBM),
    )


def shards(
    initial_thermal_state,
    logarithmic_diffusivity,
    rock_class_code,
    rock_class_diffusivity,
    advection_courant,
    probe_locations,
    observed_readings,
    probe_noise_deviation,
    random_starters,
):
    span_x, span_y, depth, members = initial_thermal_state.shape
    rows = (span_x, span_y)
    cells = span_x * span_y
    temperature = initial_thermal_state.reshape(cells, depth, members)
    log_cond = logarithmic_diffusivity.reshape(cells, depth, members)
    tile = f32(cells, depth, members)
    faces = [(span_y, depth, members)] * 2 + [(span_x, depth, members)] * 2
    levels = rock_class_diffusivity.shape
    columns = -(-cells // 128) * 128
    temperature, log_cond, base, *sent = call(
        functools.partial(prepare, rows), "prepare",
        (tile, tile, f32(depth, columns), *(f32(2, *face) for face in faces)),
        [HBM] * 4,
        [
            pltpu.with_memory_space_constraint(array, pltpu.HBM)
            for array in (temperature, log_cond, rock_class_code, rock_class_diffusivity)
        ],
        scratch=[
            pltpu.VMEM((cells, depth, members), jnp.float32),
            pltpu.VMEM((columns, 128), jnp.float32),
            pltpu.VMEM(rock_class_code.shape, jnp.int32),
            pltpu.SMEM(levels, jnp.float32),
            pltpu.SemaphoreType.DMA((5,)),
        ],
    )
    got = exchange(sent)
    half_cond, middle = call(
        functools.partial(middle_inside, rows), "middle_inside", (tile, tile),
        [SMEM] + [VMEM] * 3, [advection_courant, temperature, log_cond, base],
        flops=10**7,
    )
    middle, *sent = call(
        functools.partial(middle_border, rows), "middle_border",
        (tile, *(f32(*face) for face in faces)),
        [SMEM] + [VMEM] * 7,
        [advection_courant, temperature, half_cond, *[got[n] for n in ORDER], middle],
        flops=10**7, aliases={7: 0},
    )
    got_middle = exchange(sent)
    final = call(
        functools.partial(final_inside, rows), "final_inside", tile,
        [SMEM] + [VMEM] * 2, [advection_courant, middle, half_cond], flops=10**7,
    )
    scale = (members - 1) ** 0.5
    obs_count = probe_locations.shape[0]
    final, scaled = call(
        functools.partial(observe, rows), "observe", (tile, f32(obs_count, members)),
        [SMEM] * 4 + [VMEM] * 11,
        [
            advection_courant, probe_locations, observed_readings,
            1.0 / (probe_noise_deviation * scale), middle, half_cond, *[got_middle[n] for n in ORDER], *[got[n] for n in ORDER], final,
        ],
        flops=10**7, aliases={14: 0},
    )
    count_x, count_y = lax.axis_size("gx"), lax.axis_size("gy")
    gathers, sums = plan_exchange(count_x, count_y, obs_count, 4 * members)
    pieces, owners = gather_blocks(scaled, gathers, count_x * count_y)
    owner = jnp.asarray(owners, jnp.int32)[lax.axis_index(("gx", "gy"))]
    obs_index = (
        owner[:, None] * obs_count + jnp.arange(obs_count, dtype=jnp.int32)[None, :]
    ).reshape(-1)
    noise = inflation**0.5 * perturbation(obs_index, random_starters)
    updated, final = assimilate(
        scale, pieces, noise, log_cond.reshape(-1, members), final, sums
    )
    shape = initial_thermal_state.shape
    return (final.reshape(shape), updated.reshape(shape))


def solution(mesh):
    placed = (
        P("gx", "gy", None, None),
        P("gx", "gy", None, None),
        P("gx", "gy", None),
        P(),
        P(),
        P(("gx", "gy")),
        P(("gx", "gy")),
        P(("gx", "gy")),
        P(),
    )
    return jax.shard_map(
        shards,
        mesh=mesh,
        in_specs=placed,
        out_specs=(P("gx", "gy", None, None), P("gx", "gy", None, None)),
        check_vma=False,
    )
```
